128 devices in a mesh: strip: 32 (over y, x, core), sub: 4 (over z).
Axes of the slice: x: 4, y: 4, z: 4, core: 2. Of those that a mesh axis runs over, the one named last changes fastest.
Arguments:
- counts: int32 [1024, 32768], P('strip', 'sub'), may hold values from 0 to 5
- offset: float32 [1024, 32768], P('strip', 'sub'), may hold values from -1.2 to 1.45
- kappa: float32 [1024, 32768], P('strip', 'sub'), may hold values from 0.01 to 1
- labels: int32 [8, 256], P(None, 'sub'), may hold values from 0 to 1023
- owner: int32 [1024], replicated, may hold values from 0 to 127, as said below
Outputs:
- mode: float32 [1024, 32768], P('strip', 'sub')
- owned: float32 [1920], P(('strip', 'sub'))
The draws below stay inside these ranges and needn't reach their ends.
Inputs may be any that keep to these rules, and one draw needn't show every extreme that they name: owner of each region as an index along strip+sub (strip slowest); each device owns 1 to 15 regions, and some device exactly 15.
All inputs are finite; a program needn't handle non-finite values.
Results may differ from the reference program's by a relative error of at most 0.0001.
Values sent between devices are 32-bit elements; how exact they have to be, the bound alone decides.
A program may use at most 64 MiB of HBM per device.

```python
import math
import jax
import jax.numpy as jnp

TILE = 128
NEWTON_STEPS = 2
INNER_STEPS = 3
REGIONS_EACH = 8
REGIONS = 1024
OWNED_MOST = 15
NX = 1024
NY = 32768
DEVICES = 128


def draw_counts(key, part):
    rows = jnp.arange(NX, dtype=jnp.int32)
    ceiling = 2 + 5 * rows // NX
    return jax.random.randint(key, (NX, NY), 0, ceiling[:, None], dtype=jnp.int32)


def draw_offset(key, part):
    rows = jnp.arange(NX, dtype=jnp.float32)[:, None]
    level = jnp.log(0.5 + 2.0 * rows / NX)
    noise = jax.random.uniform(key, (NX, NY), jnp.float32, -0.5, 0.5)
    return (level + noise).astype(jnp.float32)


def draw_owner(key, part):
    first, second, third, fourth = jax.random.split(jax.random.fold_in(key, 17), 4)
    half = DEVICES // 2
    extra = jax.random.randint(first, (half,), 0, REGIONS_EACH, dtype=jnp.int32)
    forced = jax.random.randint(second, (), 0, half, dtype=jnp.int32)
    extra = jnp.where(jnp.arange(half, dtype=jnp.int32) == forced, REGIONS_EACH - 1, extra)
    load = jnp.stack([REGIONS_EACH + extra, REGIONS_EACH - extra], axis=1).reshape(DEVICES)
    load = load[jax.random.permutation(third, DEVICES)]
    ends = jnp.cumsum(load)
    listed = jnp.searchsorted(ends, jnp.arange(REGIONS_EACH * DEVICES, dtype=jnp.int32), side='right')
    return jax.random.permutation(fourth, listed.astype(jnp.int32)).astype(jnp.int32)


def plant(drawn, rng, least, high):
    place = [jax.random.randint(jax.random.fold_in(rng, axis), (), 0, length) for axis, length in enumerate(drawn.shape)]
    longest = drawn.shape.index(max(drawn.shape))
    neighbour = place[:longest] + [(place[longest] + 1) % drawn.shape[longest]] + place[longest + 1:]
    return drawn.at[tuple(place)].set(least).at[tuple(neighbour)].set(high)


def level_of(rng, extent, cuts, low, largest):
    def one(dim, parts):
        draws = jax.random.uniform(jax.random.fold_in(jax.random.fold_in(rng, 6), dim), (parts,), jnp.float32, low / len(cuts), largest / len(cuts))
        return jnp.repeat(jnp.exp(draws), extent[dim] // parts).reshape((-1,) + (1,) * (len(extent) - dim - 1))

    gain = one(*cuts[0])
    for cut in cuts[1:]:
        gain = gain * one(*cut)
    return gain


def setup_inputs(seed: int = 0) -> dict:
    streams_of = jax.random.split(jax.random.key(seed), 6)
    counts = draw_counts(jax.random.fold_in(streams_of[5], 71), 0)
    offset = draw_offset(jax.random.fold_in(streams_of[5], 71), 0)
    kappa = jnp.clip(jnp.exp(math.log(1.0) - 4.6051702 * jax.random.uniform(streams_of[2], (NX, NY), jnp.float32) ** level_of(streams_of[2], (NX, NY), ((0, 32), (1, 4)), -0.2, 0.2)), 0.01, 1.0)
    labels = plant(jax.random.randint(streams_of[3], (NX // TILE, NY // TILE), 0, REGIONS), jax.random.fold_in(streams_of[3], 1), 0, REGIONS - 1).astype(jnp.int32)
    owner = draw_owner(jax.random.fold_in(streams_of[5], 71), 0)
    return dict(counts=counts, offset=offset, kappa=kappa, labels=labels, owner=owner)


prior_scale = 0.1


def stencil(field, kappa):
    padded = jnp.pad(field, 1)
    beside_all = padded[2:, 1:-1] + padded[:-2, 1:-1] + padded[1:-1, 2:] + padded[1:-1, :-2]
    return (kappa + 4.0) * field - beside_all


def precision_apply(field, kappa):
    return prior_scale * stencil(stencil(field, kappa), kappa)


def reference(counts, offset, kappa, labels, owner):
    observed = counts.astype(jnp.float32)
    mode = jnp.zeros(offset.shape, jnp.float32)
    for newton_step in range(NEWTON_STEPS):
        weight = jnp.exp(offset + mode)
        gradient = observed - weight - precision_apply(mode, kappa)
        step = jnp.zeros(offset.shape, jnp.float32)
        residual = gradient
        direction = gradient
        norm_now = jnp.sum(residual * residual)
        for inner_step in range(INNER_STEPS):
            image = precision_apply(direction, kappa) + weight * direction
            alpha = norm_now / jnp.sum(direction * image)
            step = step + alpha * direction
            residual = residual - alpha * image
            norm_next = jnp.sum(residual * residual)
            direction = residual + (norm_next / norm_now) * direction
            norm_now = norm_next
        mode = mode + step
    intensity = jnp.exp(offset + mode)
    tile_sums = intensity.reshape(NX // TILE, TILE, NY // TILE, TILE).sum(axis=(1, 3)) / float(TILE * TILE)
    region_sums = jnp.zeros((REGIONS,), jnp.float32).at[labels.reshape(-1).astype(jnp.int32)].add(tile_sums.reshape(-1))
    marks = (owner[:, None] == jnp.arange(DEVICES, dtype=jnp.int32)[None, :]).astype(jnp.int32)
    slots = jnp.sum((jnp.cumsum(marks, axis=0) - marks) * marks, axis=1).astype(jnp.int32)
    owned = jnp.zeros((DEVICES, OWNED_MOST), jnp.float32).at[owner.astype(jnp.int32), slots].add(region_sums)
    return mode, owned.reshape(-1)
```

```python
import jax
import jax.numpy as jnp
from jax import lax
from jax.experimental import pallas as pl
from jax.experimental.pallas import tpu as pltpu
from jax.sharding import PartitionSpec as P

TILE = 128
OWNED_MOST = 15
MESH = pl.DeviceIdType.MESH
F32 = jnp.float32

ROWS, TILES, TOP, BOTTOM, SLOTS, DEEP = 32, 8, 8, 40, 48, 5
PITCH = TILES * 8
THETA = (0.0, 2.0)
SIGMA = (1.0, 2.0**-24)
TINY = 3e-7


def kernel(
    dims, counts_h, offset_h, kappa_h, labels_h, owner_h, mode_h, owned_ref,
    st_c, st_o, st_k, off_m, cnt_m, kap_m, kap_g, w_m, w_g, r_m, r_g, t_m, t_g,
    a_m, a_g, b_m, b_g, q_m, mode_m, pack, e_off, e_cnt, e_kap, e_a, e_b, e_q, e_r, e_w, e_k,
    lab, own, pick, src1, src2, got1, got2,
    ld_sem, small_sem, row_s, row_r, edge_s, edge_r, lab_s, lab_r, s1, r1, s2, r2, out_sem,
):
    strips, subs = dims
    strip, sub = lax.axis_index("strip"), lax.axis_index("sub")
    core, chip = lax.rem(strip, 2), lax.div(strip, 2)
    chips, near = strips // 2, 2 * subs
    me1 = core * subs + sub
    up, down = lax.rem(strip + strips - 1, strips), lax.rem(strip + 1, strips)
    left, right = lax.rem(sub + subs - 1, subs), lax.rem(sub + 1, subs)
    first, last = strip == 0, strip == strips - 1

    def peer1(k):
        j = lax.rem(me1 + k, near)
        return j, (strip - core + lax.div(j, subs), lax.rem(j, subs))

    def peer2(k):
        j = lax.rem(chip + k, chips)
        return j, (j * 2 + core, sub)

    def each(low, high, do):
        def step(k, carry):
            do(k)
            return carry

        lax.fori_loop(low, high, step, 0)

    barrier = pltpu.get_barrier_semaphore()

    def greet(device):
        pl.semaphore_signal(barrier, inc=1, device_id=device, device_id_type=MESH)

    each(1, near, lambda k: greet(peer1(k)[1]))
    each(1, chips, lambda k: greet(peer2(k)[1]))
    around = [
        (up, sub), (down, sub), (strip, left), (strip, right),
        (up, left), (down, left), (up, right), (down, right),
    ]
    for device in around:
        greet(device)

    order = (0, 3, 1, 2)
    loads = {}
    for i in order:
        for n, (hbm, stage) in enumerate(((offset_h, st_o), (counts_h, st_c), (kappa_h, st_k))):
            loads[i, n] = pltpu.make_async_copy(
                hbm.at[pl.ds(8 * i, 8), :], stage.at[pl.ds(8 * i, 8), :], ld_sem.at[3 * i + n]
            )
            loads[i, n].start()
    load_owner = pltpu.make_async_copy(owner_h, own, small_sem.at[0])
    load_owner.start()
    load_labels = pltpu.make_async_copy(labels_h, lab.at[sub], small_sem.at[1])
    load_labels.start()

    lane = lax.broadcasted_iota(jnp.int32, (8, 128), 1)
    sublane = lax.broadcasted_iota(jnp.int32, (8, 128), 0)

    def at(q, t):
        return pl.ds(pl.multiple_of(q * PITCH + t * 8, 8), 8)

    def ghost_at(q):
        return pl.ds(pl.multiple_of(q * 8, 8), 8)

    def relayout(i):
        for n in range(3):
            loads[i, n].wait()

        def one(s):
            for t in range(TILES):
                from_ = (pl.ds(8 * i, 8), pl.ds(pl.multiple_of(s * 1024 + t * 128, 128), 128))
                to = (pl.ds((TOP + 8 * i) * PITCH + t * 8 + s, 8, stride=PITCH), slice(None))
                off, cnt, kap = st_o[from_], st_c[from_].astype(F32), st_k[from_]
                weight = jnp.exp(off)
                off_m[to] = off
                cnt_m[to] = cnt
                kap_m[to] = kap + 4.0
                w_m[to] = weight
                r_m[to] = cnt - weight

        each(0, 8, one)

    def remote(src, dst, send, recv, device):
        return pltpu.make_async_remote_copy(
            src_ref=src, dst_ref=dst, send_sem=send, recv_sem=recv,
            device_id=device, device_id_type=MESH,
        )

    def row_copies(field, n, low, high):
        many = (high - low) * PITCH
        return [
            remote(
                field.at[pl.ds((TOP + low) * PITCH, many), :],
                field.at[pl.ds((BOTTOM + low) * PITCH, many), :],
                row_s.at[2 * n], row_r.at[2 * n], (up, sub),
            ),
            remote(
                field.at[pl.ds((BOTTOM - high) * PITCH, many), :],
                field.at[pl.ds((TOP - high) * PITCH, many), :],
                row_s.at[2 * n + 1], row_r.at[2 * n + 1], (down, sub),
            ),
        ]

    def edge_copies(leftmost, rightmost, edges, n):
        made = []
        for side, source, beside in ((1, leftmost, left), (0, rightmost, right)):
            to = edges.at[side]
            for m, (rows, landing, device) in enumerate((
                (pl.ds(0, 32), pl.ds(8, 32), (strip, beside)),
                (pl.ds(0, 8), pl.ds(40, 8), (up, beside)),
                (pl.ds(24, 8), pl.ds(0, 8), (down, beside)),
            )):
                k = 6 * n + 3 * side + m
                made.append(
                    remote(source(rows), to.at[landing, :], edge_s.at[k], edge_r.at[k], device)
                )
        return made

    def hbm_edges(hbm, edges, n):
        wide = TILES * 1024
        return edge_copies(
            lambda rows: hbm.at[rows, pl.ds(0, 128)],
            lambda rows: hbm.at[rows, pl.ds(wide - 128, 128)],
            edges, n,
        )

    def packed_edges(field, edges, n):
        for g in range(4):
            base = (TOP + 8 * g) * PITCH
            pack[n - 3, 0, pl.ds(8 * g, 8), :] = field[pl.ds(base, 8, stride=PITCH), :]
            pack[n - 3, 1, pl.ds(8 * g, 8), :] = field[pl.ds(base + PITCH - 1, 8, stride=PITCH), :]
        return edge_copies(
            lambda rows: pack.at[n - 3, 0, rows, :], lambda rows: pack.at[n - 3, 1, rows, :],
            edges, n,
        )

    def start(copies):
        for copy in copies:
            copy.start()

    def arrived(copies):
        for copy in copies:
            copy.wait_recv()

    def sent(copies):
        for copy in copies:
            copy.wait_send()

    left_open = jnp.where(sub > 0, 1.0, 0.0).astype(F32)
    right_open = jnp.where(sub < subs - 1, 1.0, 0.0).astype(F32)
    open_ = jnp.where(
        (sublane == 0) & (lane >= 64), left_open,
        jnp.where((sublane == 7) & (lane < 64), right_open, 1.0),
    )

    def row(main, ghost, q):
        return [main[at(q, t), :] for t in range(TILES)] + [ghost[ghost_at(q), :]]

    def put(main, ghost, q, values):
        for t in range(TILES):
            main[at(q, t), :] = values[t]
        ghost[ghost_at(q), :] = values[TILES]

    def stencil(above, here, below, kap):
        before = [pltpu.roll(v, 1, axis=1) for v in here]
        after = [pltpu.roll(v, 127, axis=1) for v in here]
        done = []
        for t in range(TILES + 1):
            beside = jnp.where(lane == 0, before[t - 1], before[t]) + jnp.where(
                lane == 127, after[(t + 1) % (TILES + 1)], after[t]
            )
            done.append(kap[t] * here[t] - ((above[t] + below[t]) + beside))
        done[TILES] = done[TILES] * open_
        return done

    def rows_of_k(main, ghost, q, many):
        window = [row(main, ghost, q - 1 + n) for n in range(many + 2)]
        return [
            stencil(window[n], window[n + 1], window[n + 2], row(kap_m, kap_g, q + n))
            for n in range(many)
        ], window[1:-1]

    def blank(main, ghost, low, high):
        zero = jnp.zeros((8, 128), F32)

        @pl.when(first)
        def _():
            for q in range(low, TOP):
                put(main, ghost, q, [zero] * 9)

        @pl.when(last)
        def _():
            for q in range(BOTTOM, high):
                put(main, ghost, q, [zero] * 9)

    def apply_k(main, ghost, out, out_g, low, high):
        def two(n):
            q = low + 2 * n
            made, _ = rows_of_k(main, ghost, q, 2)
            for m in range(2):
                put(out, out_g, q + m, made[m])

        each(0, (high - low) // 2, two)
        blank(out, out_g, low, high)

    def added(products):
        while len(products) > 1:
            products = [a + b for a, b in zip(products[::2], products[1::2])]
        return products[0]

    def shifted(base, base_g, out, out_g, low, high, theta, sigma, sums):
        def make(q, many):
            made, _ = rows_of_k(t_m, t_g, q, many)
            results = []
            for m in range(many):
                weight, values = row(w_m, w_g, q + m), row(base, base_g, q + m)
                got = [
                    (0.1 * sigma) * made[m][t] + (sigma * (weight[t] - theta)) * values[t]
                    for t in range(9)
                ]
                put(out, out_g, q + m, got)
                results.append((got, values))
            return results

        each(low, TOP, lambda q: make(q, 1) and None)
        each(BOTTOM, high, lambda q: make(q, 1) and None)

        def two(n, carry):
            q = TOP + 2 * n
            for m, (got, values) in enumerate(make(q, 2)):
                carry = sums(carry, got, values, q + m)
            return carry

        zero = jnp.zeros((8, 128), F32)
        total = lax.fori_loop(0, ROWS // 2, two, (zero,) * 3)
        blank(out, out_g, low, high)
        return total

    def inject(main, ghost, edges, masked=False):
        def one(q):
            ghost[ghost_at(q), :] = jnp.where(
                lane < 64,
                pltpu.roll(main[at(q, 0), :], 7, axis=0),
                pltpu.roll(main[at(q, TILES - 1), :], 1, axis=0),
            )

        each(TOP - DEEP, BOTTOM + DEEP, one)
        for g in range(SLOTS // 8):
            for side, s in ((0, 0), (1, 7)):
                where = (pl.ds(g * 64 + s, 8, stride=8), slice(None))
                mine = lane >= 64 if side == 0 else lane < 64
                fresh = edges[side, pl.ds(8 * g, 8), :]
                if masked:
                    fresh = fresh * (left_open if side == 0 else right_open)
                ghost[where] = jnp.where(mine, fresh, ghost[where])

    def hop1(u):
        def go(k):
            _, device = peer1(k)
            remote(
                src1.at[u], got1.at[near * u + me1],
                s1.at[near * u + k], r1.at[near * u + me1], device,
            ).start()

        each(1, near, go)

    def hop1_done(u):
        def wait(k):
            j, device = peer1(k)
            remote(
                src1.at[u], got1.at[near * u + j],
                s1.at[near * u + k], r1.at[near * u + j], device,
            ).wait()

        each(1, near, wait)

    def hop2(u):
        def go(k):
            _, device = peer2(k)
            remote(
                src2.at[u], got2.at[chips * u + chip],
                s2.at[chips * u + k], r2.at[chips * u + chip], device,
            ).start()

        each(1, chips, go)

    def hop2_done(u):
        def wait(k):
            j, device = peer2(k)
            remote(
                src2.at[u], got2.at[chips * u + j],
                s2.at[chips * u + k], r2.at[chips * u + j], device,
            ).wait()

        each(1, chips, wait)

    def over_sublanes(v):
        for n in (4, 2, 1):
            v = v + pltpu.roll(v, n, axis=0)
        return v

    def moments_out(u, sums):
        message = jnp.zeros((8, 128), F32)
        for n, v in enumerate(sums):
            message = jnp.where(sublane == n, over_sublanes(v), message)
        src1[u] = message
        got1[near * u + me1] = message
        hop1(u)

    def moments_on(u):
        hop1_done(u)
        total = got1[near * u]
        for j in range(1, near):
            total = total + got1[near * u + j]
        both = jnp.concatenate([total, jnp.zeros((8, 128), F32)], axis=0)
        src2[u] = both
        got2[chips * u + chip] = both
        hop2(u)

    def moments_in(u):
        hop2_done(u)
        total = got2[chips * u, 0:8, :]
        for j in range(1, chips):
            total = total + got2[chips * u + j, 0:8, :]
        flat = jnp.sum(total, axis=1, keepdims=True)
        return [jnp.broadcast_to(flat[n : n + 1, :], (8, 128)) for n in range(7)]

    def solve(moments, sigma):
        g00, g01, g11, g02, g12, g22, h22 = moments
        inverse = 1.0 / sigma
        a00 = inverse * g01 + THETA[0] * g00
        a01 = inverse * g02 + THETA[1] * g01
        a11 = inverse * g12 + THETA[1] * g11
        a02 = inverse * g12 + THETA[0] * g02
        a12 = inverse * g22 + THETA[1] * g12
        a22 = h22
        i0 = 1.0 / a00
        l10, l20 = a01 * i0, a02 * i0
        d1, u12 = a11 - l10 * a01, a12 - l10 * a02
        i1 = jnp.where(d1 > TINY * a11, 1.0 / d1, 0.0)
        l21 = u12 * i1
        d2 = a22 - l20 * a02 - l21 * u12
        i2 = jnp.where(d2 > TINY * a22, 1.0 / d2, 0.0)
        y0 = g00
        y1 = g01 - l10 * y0
        y2 = g02 - l20 * y0 - l21 * y1
        c2 = y2 * i2
        c1 = y1 * i1 - l21 * c2
        c0 = y0 * i0 - l10 * c1 - l20 * c2
        return c0, c1, c2

    relayout(order[0])
    relayout(order[1])
    pl.semaphore_wait(barrier, near - 1 + chips - 1 + len(around))
    halo = row_copies(off_m, 0, 0, 5) + row_copies(cnt_m, 1, 0, 5) + row_copies(kap_m, 2, 0, 4)
    rims = hbm_edges(offset_h, e_off, 0) + hbm_edges(counts_h, e_cnt, 1) + hbm_edges(kappa_h, e_kap, 2)
    start(halo)
    start(rims)
    load_labels.wait()

    def label_copy(k, arriving):
        z = lax.rem(sub + k, subs)
        held = z if arriving else sub
        return remote(labels_h, lab.at[held], lab_s.at[k], lab_r.at[held], (strip, z))

    for k in range(1, subs):
        label_copy(k, False).start()
    relayout(order[2])
    relayout(order[3])
    arrived(halo)
    arrived(rims)

    def halo_rows(do):
        each(TOP - DEEP, TOP, do)
        each(BOTTOM, BOTTOM + DEEP, do)

    def prime(q):
        for t in range(TILES):
            weight = jnp.exp(off_m[at(q, t), :])
            w_m[at(q, t), :] = weight
            r_m[at(q, t), :] = cnt_m[at(q, t), :] - weight

    halo_rows(prime)
    for side, alive in ((0, left_open), (1, right_open)):
        weight = jnp.exp(e_off[side])
        e_w[side] = weight
        e_r[side] = (e_cnt[side].astype(F32) - weight) * alive
        e_k[side] = e_kap[side] + 4.0
    inject(kap_m, kap_g, e_k)
    inject(w_m, w_g, e_w)
    inject(r_m, r_g, e_r)
    blank(r_m, r_g, TOP - DEEP, BOTTOM + DEEP)

    def basis(n):
        sigma = SIGMA[n]
        apply_k(r_m, r_g, t_m, t_g, 4, 44)

        def sums_a(carry, got, values, q):
            return (
                carry[0] + added([v * v for v in values[:8]]),
                carry[1] + added([v * g for v, g in zip(values[:8], got[:8])]),
                carry[2] + added([g * g for g in got[:8]]),
            )

        g00, g01, g11 = shifted(r_m, r_g, a_m, a_g, 5, 43, THETA[0], sigma, sums_a)
        moving = []
        if n == 0:
            moving = row_copies(a_m, 3, 3, 5) + packed_edges(a_m, e_a, 3)
            start(moving)
        apply_k(a_m, a_g, t_m, t_g, 6, 42)

        def sums_b(carry, got, values, q):
            start_ = row(r_m, r_g, q)
            return (
                carry[0] + added([v * g for v, g in zip(start_[:8], got[:8])]),
                carry[1] + added([v * g for v, g in zip(values[:8], got[:8])]),
                carry[2] + added([g * g for g in got[:8]]),
            )

        g02, g12, g22 = shifted(a_m, a_g, b_m, b_g, 7, 41, THETA[1], sigma, sums_b)
        if n == 0:
            more = row_copies(b_m, 4, 1, 5) + packed_edges(b_m, e_b, 4)
            start(more)
            moving = moving + more

        def energy(m, carry):
            q = TOP + 2 * m
            made, values = rows_of_k(b_m, b_g, q, 2)
            for k in range(2):
                weight = [w_m[at(q + k, t), :] for t in range(TILES)]
                carry = carry + added([
                    0.1 * (made[k][t] * made[k][t]) + weight[t] * (values[k][t] * values[k][t])
                    for t in range(TILES)
                ])
            return carry

        h22 = lax.fori_loop(0, ROWS // 2, energy, jnp.zeros((8, 128), F32))
        moments_out(n, (g00, g01, g11, g02, g12, g22, h22))
        return moving

    moving = basis(0)
    moments_on(0)

    arrived(moving)
    inject(b_m, b_g, e_b, masked=True)
    blank(b_m, b_g, TOP - DEEP, BOTTOM + DEEP)
    apply_k(b_m, b_g, t_m, t_g, 7, 41)

    def second_k(n):
        q = TOP + 2 * n
        made, _ = rows_of_k(t_m, t_g, q, 2)
        for m in range(2):
            for t in range(TILES):
                q_m[at(q + m, t), :] = 0.1 * made[m][t]

    each(0, ROWS // 2, second_k)
    final = row_copies(q_m, 5, 0, 5) + packed_edges(q_m, e_q, 5)
    start(final)
    sent(moving)

    c0, c1, c2 = solve(moments_in(0), SIGMA[0])

    def renew(off, cnt, weight, r, a, b, qb):
        step = c0 * r + (c1 * a + c2 * b)
        q_mode = c0 * (a + (THETA[0] - weight) * r) + (
            c1 * (b + (THETA[1] - weight) * a) + c2 * qb
        )
        fresh = jnp.exp(off + step)
        return step, fresh, cnt - fresh - q_mode

    def renew_row(q, keep):
        for t in range(TILES):
            k = (at(q, t), slice(None))
            step, fresh, gradient = renew(
                off_m[k], cnt_m[k], w_m[k], r_m[k], a_m[k], b_m[k], q_m[k]
            )
            if keep:
                mode_m[k] = step
            w_m[k] = fresh
            r_m[k] = gradient

    each(TOP, BOTTOM, lambda q: renew_row(q, True))
    arrived(final)
    halo_rows(lambda q: renew_row(q, False))
    for side, alive in ((0, left_open), (1, right_open)):
        for g in range(SLOTS // 8):
            k = (side, pl.ds(8 * g, 8), slice(None))
            _, fresh, gradient = renew(
                e_off[k], e_cnt[k].astype(F32), e_w[k], e_r[k], e_a[k], e_b[k], e_q[k]
            )
            e_w[k] = fresh
            e_r[k] = gradient * alive
    inject(w_m, w_g, e_w)
    inject(r_m, r_g, e_r)
    blank(r_m, r_g, TOP - DEEP, BOTTOM + DEEP)

    basis(1)
    moments_on(1)

    sent(final)
    sent(halo)
    sent(rims)
    for k in range(1, subs):
        label_copy(k, True).wait()
    load_owner.wait()
    myself = strip * subs + sub
    mark = jnp.where(own[...] == myself, 1, 0)
    count = mark
    for n in (1, 2, 4, 8, 16, 32, 64):
        count = count + jnp.where(lane >= n, pltpu.roll(count, n, axis=1), 0)
    whole = jnp.broadcast_to(count[:, 127:128], (8, 128))
    below = jnp.where(sublane >= 1, pltpu.roll(whole, 1, axis=0), 0)
    for n in (1, 2, 4):
        below = below + jnp.where(sublane >= n, pltpu.roll(below, n, axis=0), 0)
    slot = jnp.where(mark == 1, count + below - 1, -1)
    region = (sublane * 128 + lane).astype(F32)
    tiles = [
        jnp.concatenate([lab[2 * h], lab[2 * h + 1]], axis=1).astype(F32) for h in range(2)
    ]
    for s in range(OWNED_MOST):
        mine = jnp.max(jnp.where(slot == s, region, -1.0), axis=1, keepdims=True)
        mine = jnp.max(mine, axis=0, keepdims=True)
        for h in range(2):
            pick[s, pl.ds(8 * h, 8), :] = jnp.where(tiles[h] == mine, 1.0, 0.0)

    c0, c1, c2 = solve(moments_in(1), SIGMA[1])

    def finish(q, carry):
        sums = []
        for t in range(TILES):
            k = (at(q, t), slice(None))
            mode = mode_m[k] + (c0 * r_m[k] + (c1 * a_m[k] + c2 * b_m[k]))
            mode_m[k] = mode
            sums.append(carry[t] + jnp.exp(off_m[k] + mode))
        return tuple(sums)

    zero = jnp.zeros((8, 128), F32)
    sums = lax.fori_loop(TOP, BOTTOM, finish, (zero,) * TILES)
    square = zero
    for t in range(TILES):
        square = jnp.where(lane == t, jnp.sum(sums[t], axis=1, keepdims=True), square)
    line = over_sublanes(pltpu.roll(square, 0, axis=1, stride=8, stride_axis=0))
    line = jnp.where(lax.rem(sub, 2) == 1, pltpu.roll(line, 64, axis=1), line)
    message = jnp.where(sublane == lax.div(strip, TILE // ROWS), line, 0.0) * (1.0 / (TILE * TILE))
    src1[2] = message
    got1[near * 2 + me1] = message
    hop1(2)

    outs = []

    def write_out(i):
        def one(s):
            for t in range(TILES):
                st_o[pl.ds(8 * i, 8), pl.ds(pl.multiple_of(s * 1024 + t * 128, 128), 128)] = mode_m[
                    pl.ds((TOP + 8 * i) * PITCH + t * 8 + s, 8, stride=PITCH), :
                ]

        each(0, 8, one)
        outs.append(
            pltpu.make_async_copy(
                st_o.at[pl.ds(8 * i, 8), :], mode_h.at[pl.ds(8 * i, 8), :], out_sem.at[i]
            )
        )
        outs[-1].start()

    write_out(0)
    write_out(1)
    hop1_done(2)
    both = []
    for h in range(2):
        slots = [c * subs + z for c in range(2) for z in (2 * h, 2 * h + 1)]
        both.append(added([got1[near * 2 + j] for j in slots]))
    both = jnp.concatenate(both, axis=0)
    src2[2] = both
    got2[chips * 2 + chip] = both
    hop2(2)
    write_out(2)
    write_out(3)
    hop2_done(2)
    total = got2[chips * 2]
    for j in range(1, chips):
        total = total + got2[chips * 2 + j]
    answer = jnp.zeros((8, 128), F32)
    for h in range(2):
        gathered = zero
        for s in range(8 * h, min(8 * h + 8, OWNED_MOST)):
            both = total * pick[s]
            gathered = jnp.where(
                sublane == s - 8 * h, over_sublanes(both[0:8] + both[8:16]), gathered
            )
        flat = jnp.sum(gathered, axis=1, keepdims=True)
        answer = answer + jnp.where(lane == sublane + 8 * h, flat, 0.0)
    owned_ref[...] = over_sublanes(answer)[0:1, 0:OWNED_MOST]
    for copy in outs:
        copy.wait()


def solution(mesh):
    strips, subs = mesh.shape["strip"], mesh.shape["sub"]
    near, chips = 2 * subs, strips // 2

    def body(counts, offset, kappa, labels, owner):
        height, width = offset.shape
        main = pltpu.VMEM((SLOTS * PITCH, 128), F32)
        ghost = pltpu.VMEM((SLOTS * 8, 128), F32)
        edge = pltpu.VMEM((2, SLOTS, 128), F32)
        dma = pltpu.SemaphoreType.DMA
        anywhere = pl.BlockSpec(memory_space=pl.ANY)
        mode, owned = pl.pallas_call(
            lambda *refs: kernel((strips, subs), *refs),
            out_shape=(
                jax.ShapeDtypeStruct((height, width), F32),
                jax.ShapeDtypeStruct((1, OWNED_MOST), F32),
            ),
            in_specs=[anywhere] * 5,
            out_specs=(anywhere, pl.BlockSpec(memory_space=pltpu.VMEM)),
            scratch_shapes=[
                pltpu.VMEM((height, width), jnp.int32),
                pltpu.VMEM((height, width), F32),
                pltpu.VMEM((height, width), F32),
                main, main, main, ghost, main, ghost, main, ghost, main, ghost,
                main, ghost, main, ghost, main, main,
                pltpu.VMEM((3, 2, 32, 128), F32),
                edge, pltpu.VMEM((2, SLOTS, 128), jnp.int32), edge,
                edge, edge, edge, edge, edge, edge,
                pltpu.VMEM((subs, 8, labels.shape[1]), jnp.int32),
                pltpu.VMEM((8, 128), jnp.int32),
                pltpu.VMEM((OWNED_MOST, 16, 128), F32),
                pltpu.VMEM((3, 8, 128), F32),
                pltpu.VMEM((3, 16, 128), F32),
                pltpu.VMEM((3 * near, 8, 128), F32),
                pltpu.VMEM((3 * chips, 16, 128), F32),
                dma((12,)), dma((2,)), dma((12,)), dma((12,)), dma((36,)), dma((36,)),
                dma((subs,)), dma((subs,)), dma((3 * near,)), dma((3 * near,)),
                dma((3 * chips,)), dma((3 * chips,)), dma((4,)),
            ],
            compiler_params=pltpu.CompilerParams(
                collective_id=0, has_side_effects=True, vmem_limit_bytes=63 << 20
            ),
        )(counts, offset, kappa, labels, owner.reshape(8, 128))
        return mode, owned.reshape(OWNED_MOST)

    return jax.shard_map(
        body,
        mesh=mesh,
        in_specs=(P("strip", "sub"), P("strip", "sub"), P("strip", "sub"), P(None, "sub"), P()),
        out_specs=(P("strip", "sub"), P(("strip", "sub"))),
        check_vma=False,
    )
```

```python
import jax
import jax.numpy as jnp
from jax import lax
from jax.experimental import pallas as pl
from jax.experimental.pallas import tpu as pltpu
from jax.sharding import PartitionSpec as P

TILE = 128
OWNED_MOST = 15
MESH = pl.DeviceIdType.MESH
F32 = jnp.float32

ROWS, TOP, BOTTOM, SLOTS, DEEP = 32, 8, 40, 48, 5
PITCH = 80
OWN = tuple(range(8, 72, 8))
ALL = (1,) + OWN + (71,)
SHIFT = 20.0
SIGMA = (1.0, 2.0**-27)
TINY = 3e-7


def kernel(
    dims, counts_h, offset_h, kappa_h, labels_h, owner_h, mode_h, owned_ref,
    st_c, st_o, st_k, off_m, cnt_m, kap_m, w_m, r_m, t_m, a_m, b_m, q_m, mode_m,
    pack, land, edge, lab, own, pick, src1, src2, got1, got2,
    ld_sem, small_sem, row_s, row_r, edge_s, edge_r, lab_s, lab_r, s1, r1, s2, r2, out_sem,
):
    strips, subs = dims
    strip, sub = lax.axis_index("strip"), lax.axis_index("sub")
    core, chip = lax.rem(strip, 2), lax.div(strip, 2)
    chips, near = strips // 2, 2 * subs
    me1 = core * subs + sub
    up, down = lax.rem(strip + strips - 1, strips), lax.rem(strip + 1, strips)
    left, right = lax.rem(sub + subs - 1, subs), lax.rem(sub + 1, subs)
    first, last = strip == 0, strip == strips - 1

    def far(n, size):
        return min(n, size - n)

    peers1 = []
    for flip, dz in sorted(
        ((f, d) for f in range(2) for d in range(subs) if f or d),
        key=lambda v: (-far(v[1], subs), -v[0]),
    ):
        other, z = (1 - core if flip else core), lax.rem(sub + dz, subs)
        peers1.append((other * subs + z, (chip * 2 + other, z)))
    side = 4 if chips == 16 else 2
    tall = chips // side
    peers2 = []
    for dy, dx in sorted(
        ((y, x) for y in range(tall) for x in range(side) if y or x),
        key=lambda v: -far(v[0], tall) - far(v[1], side),
    ):
        j = lax.rem(lax.div(chip, side) + dy, tall) * side + lax.rem(lax.rem(chip, side) + dx, side)
        peers2.append((j, (j * 2 + core, sub)))

    def each(low, high, do):
        def step(k, carry):
            do(k)
            return carry

        lax.fori_loop(low, high, step, 0)

    barrier = pltpu.get_barrier_semaphore()
    around = [
        (up, sub), (down, sub), (strip, left), (strip, right),
        (up, left), (down, left), (up, right), (down, right),
    ]
    greeted = [device for _, device in peers2 + peers1] + around
    for device in greeted:
        pl.semaphore_signal(barrier, inc=1, device_id=device, device_id_type=MESH)

    order = (0, 3, 1, 2)
    loads = {}
    for i in order:
        for n, (hbm, stage) in enumerate(((offset_h, st_o), (counts_h, st_c), (kappa_h, st_k))):
            part = pl.ds(512 * i, 512)
            loads[i, n] = pltpu.make_async_copy(hbm.at[part, :], stage.at[part, :], ld_sem.at[3 * i + n])
            loads[i, n].start()
    load_owner = pltpu.make_async_copy(owner_h, own, small_sem.at[0])
    load_owner.start()
    load_labels = pltpu.make_async_copy(labels_h, lab.at[sub], small_sem.at[1])
    load_labels.start()

    lane = lax.broadcasted_iota(jnp.int32, (8, 128), 1)
    sublane = lax.broadcasted_iota(jnp.int32, (8, 128), 0)
    low_half = lane < 64
    zero = jnp.zeros((8, 128), F32)

    def relayout(i, wait=True):
        for n in range(3 if wait else 0):
            loads[i, n].wait()

        def pair(m):
            row = 2 * m

            def turned(stage):
                x = [
                    [
                        stage[pl.ds(512 * i + 64 * g + row + d, 8, stride=8), :].astype(F32)
                        for g in range(8)
                    ]
                    for d in range(2)
                ]
                upper = [jnp.where(low_half, x[0][g], pltpu.roll(x[1][g], 64, axis=1)) for g in range(8)]
                lower = [jnp.where(low_half, pltpu.roll(x[0][g], 64, axis=1), x[1][g]) for g in range(8)]
                return jnp.concatenate(upper + lower, axis=0).T

            off, cnt, kap = turned(st_o), turned(st_c), turned(st_k)
            for d in range(2):
                q = TOP + 8 * i + row + d
                part = slice(64 * d, 64 * d + 64)
                weight = jnp.exp(off[part])
                off_m[q, 8:72, :] = off[part]
                cnt_m[q, 8:72, :] = cnt[part]
                kap_m[q, 8:72, :] = kap[part] + 4.0
                w_m[q, 8:72, :] = 10.0 * weight
                r_m[q, 8:72, :] = cnt[part] - weight

        each(0, 4, pair)

    def remote(src, dst, send, recv, device):
        return pltpu.make_async_remote_copy(
            src_ref=src, dst_ref=dst, send_sem=send, recv_sem=recv,
            device_id=device, device_id_type=MESH,
        )

    def row_copies(field, n, low, high):
        many = high - low

        def rows(q):
            return field.at[pl.ds(q, many), pl.ds(8, 64), :]

        return [
            remote(rows(TOP + low), rows(BOTTOM + low), row_s.at[2 * n], row_r.at[2 * n], (up, sub)),
            remote(
                rows(BOTTOM - high), rows(TOP - high),
                row_s.at[2 * n + 1], row_r.at[2 * n + 1], (down, sub),
            ),
        ]

    def edge_copies(n):
        made = []
        for to, beside in ((1, left), (0, right)):
            for m, device in enumerate(((strip, beside), (down, beside), (up, beside))):
                k = 6 * n + 3 * to + m
                made.append(
                    remote(pack.at[n, to], land.at[k], edge_s.at[k], edge_r.at[k], device)
                )
        return made

    def pack_field(field, n):
        tiles = [zero, zero]
        for q in range(TOP, BOTTOM):
            for to, p, l in ((1, 8, 0), (0, 64, 127)):
                moved = pltpu.roll(field[q, p : p + 8, :], (q - l) % 128, axis=1)
                tiles[to] = jnp.where(lane == q, moved, tiles[to])
        for to in range(2):
            pack[n, to] = tiles[to]

    def pack_stage(stage, n):
        for to, g, keep in ((1, 0, slice(0, 8)), (0, 63, slice(120, 128))):
            x = [stage[pl.ds(512 * i + 8 * g, 8), :].astype(F32) for i in range(4)]
            pack[n, to] = jnp.concatenate([zero] + x + [zero] * 11, axis=0).T[keep]

    def landed(n, to):
        k = 6 * n + 3 * to
        return jnp.where(
            lane < TOP, pltpu.roll(land[k + 1], 96, axis=1),
            jnp.where(lane < BOTTOM, land[k], pltpu.roll(land[k + 2], 32, axis=1)),
        )

    def start(copies):
        for copy in copies:
            copy.start()

    def arrived(copies):
        for copy in copies:
            copy.wait_recv()

    def sent(copies):
        for copy in copies:
            copy.wait_send()

    left_open = jnp.where(sub > 0, 1.0, 0.0).astype(F32)
    right_open = jnp.where(sub < subs - 1, 1.0, 0.0).astype(F32)
    left_shut = jnp.where((lane == 0) & (sublane < 7), 1.0 - left_open, 0.0) > 0.5
    right_shut = jnp.where((lane == 127) & (sublane >= 1), 1.0 - right_open, 0.0) > 0.5

    def at(field, q, p):
        return field[q, p : p + 8, :]

    def put(field, q, p, value):
        field[q, p : p + 8, :] = value

    def k_tile(field, q, p, many):
        window = [at(field, q - 1 + m, p) for m in range(many + 2)]
        made = []
        for m in range(many):
            beside = at(field, q + m, p - 1) + at(field, q + m, p + 1)
            value = at(kap_m, q + m, p) * window[m + 1] - ((window[m] + window[m + 2]) + beside)
            if p == ALL[0]:
                value = jnp.where(left_shut, 0.0, value)
            if p == ALL[-1]:
                value = jnp.where(right_shut, 0.0, value)
            made.append(value)
        return made, window[1:-1]

    def blank(field, low, high):
        nothing = jnp.zeros((PITCH, 128), F32)

        @pl.when(first)
        def _():
            for q in range(low, TOP):
                field[q] = nothing

        @pl.when(last)
        def _():
            for q in range(BOTTOM, high):
                field[q] = nothing

    def blocks(low, high, many, do):
        each(0, (high - low) // many, lambda n: do(low + many * n))

    def apply_k(field, out, low, high, many):
        def block(q):
            for p in ALL:
                made, _ = k_tile(field, q, p, many)
                for m in range(many):
                    put(out, q + m, p, made[m])

        blocks(low, high, many, block)
        blank(out, low, high)

    def shifted(base, out, low, high, shift, sigma, products):
        def block(q, many, carry):
            for p in ALL:
                made, _ = k_tile(t_m, q, p, many)
                for m in range(many):
                    value, weight = at(base, q + m, p), at(w_m, q + m, p)
                    if shift:
                        weight = weight - sigma * shift
                    got = (made[m] if sigma == 1.0 else sigma * made[m]) + weight * value
                    put(out, q + m, p, got)
                    if carry is not None and p in OWN:
                        terms = products(q + m, p, value, got)
                        h = (p // 8) % 2
                        carry[h] = [c + x for c, x in zip(carry[h], terms)]
            return carry

        each(low, TOP, lambda q: block(q, 1, None) and None)
        each(BOTTOM, high, lambda q: block(q, 1, None) and None)
        count = len(products(TOP, 8, zero, zero))

        def some(n, carry):
            got = block(TOP + 2 * n, 2, [list(carry[:count]), list(carry[count:])])
            return tuple(got[0] + got[1])

        total = lax.fori_loop(0, ROWS // 2, some, (zero,) * (2 * count))
        blank(out, low, high)
        return [total[k] + total[count + k] for k in range(count)]

    def inject(field, edges):
        for q in range(TOP - DEEP, BOTTOM + DEEP):
            x = at(field, q, 64)
            ghost = jnp.where(low_half, pltpu.roll(x, 65, axis=1), pltpu.roll(x, 64, axis=1))
            put(field, q, 0, jnp.where(lane == 0, pltpu.roll(edges[0], (128 - q) % 128, axis=1), ghost))
            x = at(field, q, 8)
            ghost = jnp.where(low_half, pltpu.roll(x, 64, axis=1), pltpu.roll(x, 63, axis=1))
            put(field, q, 72, jnp.where(lane == 127, pltpu.roll(edges[1], 127 - q, axis=1), ghost))

    def hop(peers, src, got, send, recv, size, mine, u):
        for m, (_, device) in enumerate(peers):
            remote(src.at[u], got.at[size * u + mine], send.at[size * u + m], recv.at[size * u + mine], device).start()

    def hop_done(peers, src, got, send, recv, size, u):
        for m, (slot, device) in enumerate(peers):
            remote(src.at[u], got.at[size * u + slot], send.at[size * u + m], recv.at[size * u + slot], device).wait()

    def hop1(u, message):
        src1[u] = message
        got1[near * u + me1] = message
        hop(peers1, src1, got1, s1, r1, near, me1, u)

    def hop2(u, message):
        src2[u] = message
        got2[chips * u + chip] = message
        hop(peers2, src2, got2, s2, r2, chips, chip, u)

    def added(terms):
        while len(terms) > 1:
            terms = [a + b for a, b in zip(terms[::2], terms[1::2])] + terms[len(terms) // 2 * 2 :]
        return terms[0]

    def over_sublanes(v):
        for n in (4, 2, 1):
            v = v + pltpu.roll(v, n, axis=0)
        return v

    def moments_out(u, sums):
        message = zero
        for n, v in enumerate(sums):
            message = jnp.where(sublane == n, over_sublanes(v), message)
        hop1(u, message)

    def moments_on(u):
        hop_done(peers1, src1, got1, s1, r1, near, u)
        total = added([got1[near * u + j] for j in range(near)])
        hop2(u, jnp.concatenate([total, zero], axis=0))

    def moments_in(u):
        hop_done(peers2, src2, got2, s2, r2, chips, u)
        total = added([got2[chips * u + j, 0:8, :] for j in range(chips)])
        flat = jnp.sum(total, axis=1, keepdims=True)
        return [jnp.broadcast_to(flat[n : n + 1, :], (8, 128)) for n in range(6)]

    def solve(moments, sigma):
        g00, g01, g11, g12, g22, h22 = moments
        inverse = 1.0 / sigma
        a00 = inverse * g01
        a01 = inverse * g11
        a02 = inverse * g12
        a11 = a02 + SHIFT * g11
        a12 = inverse * g22 + SHIFT * g12
        a22 = inverse * h22
        i0 = 1.0 / a00
        l10, l20 = a01 * i0, a02 * i0
        d1, u12 = a11 - l10 * a01, a12 - l10 * a02
        i1 = jnp.where(d1 > TINY * a11, 1.0 / d1, 0.0)
        l21 = u12 * i1
        d2 = a22 - l20 * a02 - l21 * u12
        i2 = jnp.where(d2 > TINY * a22, 1.0 / d2, 0.0)
        y0 = 10.0 * g00
        y1 = 10.0 * g01 - l10 * y0
        y2 = 10.0 * (g11 - (sigma * SHIFT) * g01) - l20 * y0 - l21 * y1
        c2 = y2 * i2
        c1 = y1 * i1 - l21 * c2
        c0 = y0 * i0 - l10 * c1 - l20 * c2
        return c0, c1, c2

    relayout(order[0])
    relayout(order[1])
    for i in (1, 2):
        for n in range(3):
            loads[i, n].wait()
    for n, stage in enumerate((st_o, st_c, st_k)):
        pack_stage(stage, n)
    pl.semaphore_wait(barrier, len(greeted))
    halo = []
    for n in range(3):
        halo += edge_copies(n)
    halo += row_copies(off_m, 0, 0, 5) + row_copies(cnt_m, 1, 0, 5) + row_copies(kap_m, 2, 0, 4)
    start(halo)
    load_labels.wait()

    def label_copy(k, arriving):
        z = lax.rem(sub + k, subs)
        held = z if arriving else sub
        return remote(labels_h, lab.at[held], lab_s.at[k], lab_r.at[held], (strip, z))

    for k in range(1, subs):
        label_copy(k, False).start()
    relayout(order[2], False)
    relayout(order[3], False)
    arrived(halo)

    def halo_rows(do):
        each(TOP - DEEP, TOP, do)
        each(BOTTOM, BOTTOM + DEEP, do)

    def prime(q):
        for p in OWN:
            weight = jnp.exp(at(off_m, q, p))
            put(w_m, q, p, 10.0 * weight)
            put(r_m, q, p, at(cnt_m, q, p) - weight)

    halo_rows(prime)
    alive = (left_open, right_open)
    e_off = [landed(0, to) for to in range(2)]
    e_cnt = [landed(1, to) for to in range(2)]
    e_kap = [landed(2, to) + 4.0 for to in range(2)]
    e_w = [jnp.exp(v) for v in e_off]
    e_r = [(cnt - weight) * live for cnt, weight, live in zip(e_cnt, e_w, alive)]
    e_w = [10.0 * v for v in e_w]
    inject(kap_m, e_kap)
    inject(w_m, e_w)
    inject(r_m, e_r)
    blank(r_m, TOP - DEEP, BOTTOM + DEEP)
    for to in range(2):
        for n, v in enumerate((e_off[to], e_cnt[to], e_w[to], e_r[to])):
            edge[2 * n + to] = v

    def basis(n):
        sigma = SIGMA[n]
        apply_k(r_m, t_m, 4, 44, 4)
        g00, g01, g11 = shifted(
            r_m, a_m, 5, 43, 0.0, sigma, lambda q, p, r, a: (r * r, r * a, a * a)
        )
        moving = []
        if n == 0:
            pack_field(a_m, 3)
            moving = edge_copies(3) + row_copies(a_m, 3, 3, 5)
            start(moving)
        apply_k(a_m, t_m, 6, 42, 4)
        g12, g22 = shifted(a_m, b_m, 7, 41, SHIFT, sigma, lambda q, p, a, b: (a * b, b * b))
        if n == 0:
            pack_field(b_m, 4)
            more = edge_copies(4) + row_copies(b_m, 4, 1, 5)
            start(more)
            moving = moving + more

        def energy(m, carry):
            carry = list(carry)
            q = TOP + 4 * m
            for p in OWN:
                made, values = k_tile(b_m, q, p, 4)
                for k in range(4):
                    square = made[k] * made[k]
                    carry[k % 2] = carry[k % 2] + (
                        (square if sigma == 1.0 else sigma * square)
                        + at(w_m, q + k, p) * (values[k] * values[k])
                    )
            return tuple(carry)

        h22 = added(list(lax.fori_loop(0, ROWS // 4, energy, (zero, zero))))
        moments_out(n, (g00, g01, g11, g12, g22, h22))
        return moving

    moving = basis(0)
    moments_on(0)

    arrived(moving)
    e_a = [landed(3, to) for to in range(2)]
    e_b = [landed(4, to) for to in range(2)]
    inject(b_m, [v * live for v, live in zip(e_b, alive)])
    blank(b_m, TOP - DEEP, BOTTOM + DEEP)
    apply_k(b_m, t_m, 7, 41, 2)

    def second_k(q):
        for p in OWN:
            made, _ = k_tile(t_m, q, p, 4)
            for m in range(4):
                put(q_m, q + m, p, made[m])

    blocks(TOP, BOTTOM, 4, second_k)
    pack_field(q_m, 5)
    final = edge_copies(5) + row_copies(q_m, 5, 0, 5)
    start(final)
    sent(moving)

    c0, c1, c2 = solve(moments_in(0), SIGMA[0])
    d0, d1, d2 = 0.1 * c0, 0.1 * c1, 0.1 * c2

    def renew(off, cnt, weight, r, a, b, qb):
        step = c0 * r + (c1 * a + c2 * b)
        q_mode = d0 * (a - weight * r) + (d1 * (b + (SHIFT - weight) * a) + d2 * qb)
        fresh = jnp.exp(off + step)
        return step, (10.0 * SIGMA[1]) * fresh, cnt - fresh - q_mode

    def renew_row(q, keep):
        for p in OWN:
            step, fresh, gradient = renew(*(at(f, q, p) for f in (off_m, cnt_m, w_m, r_m, a_m, b_m, q_m)))
            if keep:
                put(mode_m, q, p, step)
            put(w_m, q, p, fresh)
            put(r_m, q, p, gradient)

    each(TOP, BOTTOM, lambda q: renew_row(q, True))
    arrived(final)
    halo_rows(lambda q: renew_row(q, False))
    e_w, e_r = [], []
    for to in range(2):
        _, fresh, gradient = renew(
            edge[to], edge[2 + to], edge[4 + to], edge[6 + to], e_a[to], e_b[to], landed(5, to)
        )
        e_w.append(fresh)
        e_r.append(gradient * alive[to])
    inject(w_m, e_w)
    inject(r_m, e_r)
    blank(r_m, TOP - DEEP, BOTTOM + DEEP)

    basis(1)
    moments_on(1)

    sent(final)
    sent(halo)
    for k in range(1, subs):
        label_copy(k, True).wait()
    load_owner.wait()
    myself = strip * subs + sub
    mark = jnp.where(own[...] == myself, 1, 0)
    count = mark
    for n in (1, 2, 4, 8, 16, 32, 64):
        count = count + jnp.where(lane >= n, pltpu.roll(count, n, axis=1), 0)
    whole = jnp.broadcast_to(count[:, 127:128], (8, 128))
    below = jnp.where(sublane >= 1, pltpu.roll(whole, 1, axis=0), 0)
    for n in (1, 2, 4):
        below = below + jnp.where(sublane >= n, pltpu.roll(below, n, axis=0), 0)
    slot = jnp.where(mark == 1, count + below - 1, -1)
    region = (sublane * 128 + lane).astype(F32)
    tiles = [
        jnp.concatenate([lab[2 * h], lab[2 * h + 1]], axis=1).astype(F32) for h in range(2)
    ]
    for s in range(OWNED_MOST):
        mine = jnp.max(jnp.where(slot == s, region, -1.0), axis=1, keepdims=True)
        mine = jnp.max(mine, axis=0, keepdims=True)
        for h in range(2):
            pick[s, pl.ds(8 * h, 8), :] = jnp.where(tiles[h] == mine, 1.0, 0.0)

    c0, c1, c2 = solve(moments_in(1), SIGMA[1])

    def finish(q, carry):
        sums = list(carry)
        for p in OWN:
            mode = at(mode_m, q, p) + (c0 * at(r_m, q, p) + (c1 * at(a_m, q, p) + c2 * at(b_m, q, p)))
            put(mode_m, q, p, mode)
            h = (p // 8) % 4
            sums[h] = sums[h] + jnp.exp(at(off_m, q, p) + mode)
        return tuple(sums)

    line = over_sublanes(added(list(lax.fori_loop(TOP, BOTTOM, finish, (zero,) * 4))))
    line = line + pltpu.roll(line, 64, axis=1)
    mine = (sublane == lax.div(strip, TILE // ROWS)) & (lax.div(lane, 64) == lax.rem(sub, 2))
    hop1(2, jnp.where(mine, line * (1.0 / (TILE * TILE)), 0.0))

    outs = []

    def write_out(i):
        def pair(m):
            row = 2 * m
            q = TOP + 8 * i + row
            x = jnp.concatenate([mode_m[q, 8:72, :], mode_m[q + 1, 8:72, :]], axis=0).T
            for g in range(8):
                upper, lower = x[8 * g : 8 * g + 8], x[64 + 8 * g : 72 + 8 * g]
                to = 512 * i + 64 * g + row
                st_o[pl.ds(to, 8, stride=8), :] = jnp.where(low_half, upper, pltpu.roll(lower, 64, axis=1))
                st_o[pl.ds(to + 1, 8, stride=8), :] = jnp.where(low_half, pltpu.roll(upper, 64, axis=1), lower)

        each(0, 4, pair)
        part = pl.ds(512 * i, 512)
        outs.append(pltpu.make_async_copy(st_o.at[part, :], mode_h.at[part, :], out_sem.at[i]))
        outs[-1].start()

    write_out(0)
    write_out(1)
    hop_done(peers1, src1, got1, s1, r1, near, 2)
    both = []
    for h in range(2):
        slots = [c * subs + z for c in range(2) for z in (2 * h, 2 * h + 1)]
        both.append(added([got1[near * 2 + j] for j in slots]))
    hop2(2, jnp.concatenate(both, axis=0))
    write_out(2)
    write_out(3)
    hop_done(peers2, src2, got2, s2, r2, chips, 2)
    total = added([got2[chips * 2 + j] for j in range(chips)])
    answer = zero
    for h in range(2):
        gathered = zero
        for s in range(8 * h, min(8 * h + 8, OWNED_MOST)):
            both = total * pick[s]
            gathered = jnp.where(
                sublane == s - 8 * h, over_sublanes(both[0:8] + both[8:16]), gathered
            )
        flat = jnp.sum(gathered, axis=1, keepdims=True)
        answer = answer + jnp.where(lane == sublane + 8 * h, flat, 0.0)
    owned_ref[...] = over_sublanes(answer)[0:1, 0:OWNED_MOST]
    for copy in outs:
        copy.wait()


def solution(mesh):
    strips, subs = mesh.shape["strip"], mesh.shape["sub"]
    near, chips = 2 * subs, strips // 2

    def tiled(x):
        return x.reshape(4, 8, 64, 128).transpose(0, 2, 1, 3).reshape(2048, 128)

    def body(counts, offset, kappa, labels, owner):
        field = pltpu.VMEM((SLOTS, PITCH, 128), F32)
        stage = pltpu.VMEM((2048, 128), F32)
        dma = pltpu.SemaphoreType.DMA
        anywhere = pl.BlockSpec(memory_space=pl.ANY)
        mode, owned = pl.pallas_call(
            lambda *refs: kernel((strips, subs), *refs),
            out_shape=(
                jax.ShapeDtypeStruct((2048, 128), F32),
                jax.ShapeDtypeStruct((1, OWNED_MOST), F32),
            ),
            in_specs=[anywhere] * 5,
            out_specs=(anywhere, pl.BlockSpec(memory_space=pltpu.VMEM)),
            scratch_shapes=[
                pltpu.VMEM((2048, 128), jnp.int32), stage, stage,
                field, field, field, field, field, field, field, field, field, field,
                pltpu.VMEM((6, 2, 8, 128), F32),
                pltpu.VMEM((36, 8, 128), F32),
                pltpu.VMEM((8, 8, 128), F32),
                pltpu.VMEM((subs, 8, labels.shape[1]), jnp.int32),
                pltpu.VMEM((8, 128), jnp.int32),
                pltpu.VMEM((OWNED_MOST, 16, 128), F32),
                pltpu.VMEM((3, 8, 128), F32),
                pltpu.VMEM((3, 16, 128), F32),
                pltpu.VMEM((3 * near, 8, 128), F32),
                pltpu.VMEM((3 * chips, 16, 128), F32),
                dma((12,)), dma((2,)), dma((12,)), dma((12,)), dma((36,)), dma((36,)),
                dma((subs,)), dma((subs,)), dma((3 * near,)), dma((3 * near,)),
                dma((3 * chips,)), dma((3 * chips,)), dma((4,)),
            ],
            compiler_params=pltpu.CompilerParams(
                collective_id=0, has_side_effects=True, vmem_limit_bytes=63 << 20
            ),
        )(tiled(counts), tiled(offset), tiled(kappa), labels, owner.reshape(8, 128))
        mode = mode.reshape(4, 64, 8, 128).transpose(0, 2, 1, 3).reshape(32, 8192)
        return mode, owned.reshape(OWNED_MOST)

    return jax.shard_map(
        body,
        mesh=mesh,
        in_specs=(P("strip", "sub"), P("strip", "sub"), P("strip", "sub"), P(None, "sub"), P()),
        out_specs=(P("strip", "sub"), P(("strip", "sub"))),
        check_vma=False,
    )
```

```python
import jax
import jax.numpy as jnp
from jax import lax
from jax.experimental import pallas as pl
from jax.experimental.pallas import tpu as pltpu
from jax.sharding import PartitionSpec as P

TILE = 128
OWNED_MOST = 15
MESH = pl.DeviceIdType.MESH
F32 = jnp.float32

ROWS, TOP, BOTTOM, SLOTS, DEEP = 32, 8, 40, 48, 5
PITCH = 80
OWN = tuple(range(8, 72, 8))
ALL = (1,) + OWN + (71,)
SHIFTS = (3.0, 40.0)
SIGMA = (1.0, 2.0**-27)
TINY = 3e-7


def kernel(
    dims, counts_h, offset_h, kappa_h, labels_h, owner_h, mode_h, owned_ref,
    st_c, st_o, st_k, off_m, kap_m, w_m, r_m, t_m, a_m, b_m, q_m, mode_m,
    pack, land, lab, own, pick, src1, src2, got1, got2,
    ld_sem, small_sem, row_s, row_r, edge_s, edge_r, lab_s, lab_r, s1, r1, s2, r2, out_sem,
):
    strips, subs = dims
    strip, sub = lax.axis_index("strip"), lax.axis_index("sub")
    core, chip = lax.rem(strip, 2), lax.div(strip, 2)
    chips, near = strips // 2, 2 * subs
    me1 = core * subs + sub
    up, down = lax.rem(strip + strips - 1, strips), lax.rem(strip + 1, strips)
    left, right = lax.rem(sub + subs - 1, subs), lax.rem(sub + 1, subs)
    first, last = strip == 0, strip == strips - 1

    def far(n, size):
        return min(n, size - n)

    peers1 = []
    for flip, dz in sorted(
        ((f, d) for f in range(2) for d in range(subs) if f or d),
        key=lambda v: (-far(v[1], subs), -v[0]),
    ):
        other, z = (1 - core if flip else core), lax.rem(sub + dz, subs)
        peers1.append((other * subs + z, (chip * 2 + other, z)))
    side = 4 if chips == 16 else 2
    tall = chips // side
    peers2 = []
    for dy, dx in sorted(
        ((y, x) for y in range(tall) for x in range(side) if y or x),
        key=lambda v: -far(v[0], tall) - far(v[1], side),
    ):
        j = lax.rem(lax.div(chip, side) + dy, tall) * side + lax.rem(lax.rem(chip, side) + dx, side)
        peers2.append((j, (j * 2 + core, sub)))

    def each(low, high, do):
        def step(k, carry):
            do(k)
            return carry

        lax.fori_loop(low, high, step, 0)

    barrier = pltpu.get_barrier_semaphore()
    around = [
        (up, sub), (down, sub), (strip, left), (strip, right),
        (up, left), (down, left), (up, right), (down, right),
    ]
    greeted = [device for _, device in peers2 + peers1] + around
    for device in greeted:
        pl.semaphore_signal(barrier, inc=1, device_id=device, device_id_type=MESH)

    order = (0, 3, 1, 2)
    loads = {}
    for i in order:
        for n, (hbm, stage) in enumerate(((offset_h, st_o), (counts_h, st_c), (kappa_h, st_k))):
            part = pl.ds(512 * i, 512)
            loads[i, n] = pltpu.make_async_copy(hbm.at[part, :], stage.at[part, :], ld_sem.at[3 * i + n])
            loads[i, n].start()
    load_owner = pltpu.make_async_copy(owner_h, own, small_sem.at[0])
    load_owner.start()
    load_labels = pltpu.make_async_copy(labels_h, lab.at[sub], small_sem.at[1])
    load_labels.start()

    lane = lax.broadcasted_iota(jnp.int32, (8, 128), 1)
    sublane = lax.broadcasted_iota(jnp.int32, (8, 128), 0)
    low_half = lane < 64
    zero = jnp.zeros((8, 128), F32)

    def relayout(i, wait=True):
        for n in range(3 if wait else 0):
            loads[i, n].wait()

        def pair(m):
            row = 2 * m

            def turned(stage):
                x = [
                    [
                        stage[pl.ds(512 * i + 64 * g + row + d, 8, stride=8), :].astype(F32)
                        for g in range(8)
                    ]
                    for d in range(2)
                ]
                upper = [jnp.where(low_half, x[0][g], pltpu.roll(x[1][g], 64, axis=1)) for g in range(8)]
                lower = [jnp.where(low_half, pltpu.roll(x[0][g], 64, axis=1), x[1][g]) for g in range(8)]
                return jnp.concatenate(upper + lower, axis=0).T

            off, cnt, kap = turned(st_o), turned(st_c), turned(st_k)
            for d in range(2):
                q = TOP + 8 * i + row + d
                part = slice(64 * d, 64 * d + 64)
                weight = jnp.exp(off[part])
                off_m[q, 8:72, :] = off[part]
                kap_m[q, 8:72, :] = kap[part] + 4.0
                w_m[q, 8:72, :] = 10.0 * weight
                r_m[q, 8:72, :] = cnt[part] - weight

        each(0, 4, pair)

    def remote(src, dst, send, recv, device):
        return pltpu.make_async_remote_copy(
            src_ref=src, dst_ref=dst, send_sem=send, recv_sem=recv,
            device_id=device, device_id_type=MESH,
        )

    def row_copies(field, n, low, high):
        many = high - low

        def rows(q):
            return field.at[pl.ds(q, many), pl.ds(8, 64), :]

        return [
            remote(rows(TOP + low), rows(BOTTOM + low), row_s.at[2 * n], row_r.at[2 * n], (up, sub)),
            remote(
                rows(BOTTOM - high), rows(TOP - high),
                row_s.at[2 * n + 1], row_r.at[2 * n + 1], (down, sub),
            ),
        ]

    def edge_copies(n):
        made = []
        for to, beside in ((1, left), (0, right)):
            for m, device in enumerate(((strip, beside), (down, beside), (up, beside))):
                k = 6 * n + 3 * to + m
                made.append(
                    remote(pack.at[n, to], land.at[k], edge_s.at[k], edge_r.at[k], device)
                )
        return made

    def pack_field(field, n):
        tiles = [zero, zero]
        for q in range(TOP, BOTTOM):
            for to, p, l in ((1, 8, 0), (0, 64, 127)):
                moved = pltpu.roll(field[q, p : p + 8, :], (q - l) % 128, axis=1)
                tiles[to] = jnp.where(lane == q, moved, tiles[to])
        for to in range(2):
            pack[n, to] = tiles[to]

    def pack_inputs():
        for to, g, keep in ((1, 0, slice(0, 8)), (0, 63, slice(120, 128))):
            tiles = []
            for stage in (st_o, st_c, st_k):
                x = [stage[pl.ds(512 * i + 8 * g, 8), :].astype(F32) for i in range(4)]
                tiles.append(jnp.concatenate([zero] + x + [zero] * 11, axis=0).T[keep])
            pack[0, to] = tiles[0]
            pack[1, to] = tiles[1] - jnp.exp(tiles[0])
            pack[2, to] = tiles[2]

    def landed(n, to):
        k = 6 * n + 3 * to
        return jnp.where(
            lane < TOP, pltpu.roll(land[k + 1], 96, axis=1),
            jnp.where(lane < BOTTOM, land[k], pltpu.roll(land[k + 2], 32, axis=1)),
        )

    def start(copies):
        for copy in copies:
            copy.start()

    def arrived(copies):
        for copy in copies:
            copy.wait_recv()

    def sent(copies):
        for copy in copies:
            copy.wait_send()

    left_open = jnp.where(sub > 0, 1.0, 0.0).astype(F32)
    right_open = jnp.where(sub < subs - 1, 1.0, 0.0).astype(F32)
    left_shut = jnp.where((lane == 0) & (sublane < 7), 1.0 - left_open, 0.0) > 0.5
    right_shut = jnp.where((lane == 127) & (sublane >= 1), 1.0 - right_open, 0.0) > 0.5

    def at(field, q, p):
        return field[q, p : p + 8, :]

    def put(field, q, p, value):
        field[q, p : p + 8, :] = value

    def k_tile(field, q, p, many):
        window = [at(field, q - 1 + m, p) for m in range(many + 2)]
        made = []
        for m in range(many):
            beside = at(field, q + m, p - 1) + at(field, q + m, p + 1)
            value = at(kap_m, q + m, p) * window[m + 1] - ((window[m] + window[m + 2]) + beside)
            if p == ALL[0]:
                value = jnp.where(left_shut, 0.0, value)
            if p == ALL[-1]:
                value = jnp.where(right_shut, 0.0, value)
            made.append(value)
        return made, window[1:-1]

    def blank(field, low, high):
        nothing = jnp.zeros((PITCH, 128), F32)

        @pl.when(first)
        def _():
            for q in range(low, TOP):
                field[q] = nothing

        @pl.when(last)
        def _():
            for q in range(BOTTOM, high):
                field[q] = nothing

    def blocks(low, high, many, do):
        each(0, (high - low) // many, lambda n: do(low + many * n))

    def k_block(field, out, q, many):
        for p in ALL:
            made, _ = k_tile(field, q, p, many)
            for m in range(many):
                put(out, q + m, p, made[m])

    def apply_k(field, out, low, high, many):
        blocks(low, high, many, lambda q: k_block(field, out, q, many))

    def summed(sums, n, terms):
        sums[n % 2] = [x + y for x, y in zip(sums[n % 2], terms)]

    def shift_block(base, out, q, many, shift, sigma, products, sums, counted):
        for p in ALL:
            made, _ = k_tile(t_m, q, p, many)
            for m in range(many):
                value, weight = at(base, q + m, p), at(w_m, q + m, p)
                got = (made[m] if sigma == 1.0 else sigma * made[m]) + (weight - sigma * shift) * value
                put(out, q + m, p, got)
                if m in counted and p in OWN:
                    summed(sums, m + p // 8, products(value, got))

    def energy_block(q, many, sigma, sums):
        for p in OWN:
            made, values = k_tile(b_m, q, p, many)
            for m in range(many):
                square = made[m] * made[m]
                square = square if sigma == 1.0 else sigma * square
                summed(sums, m + p // 8, [square + at(w_m, q + m, p) * (values[m] * values[m])])

    def sum_blocks(low, high, many, count, do):
        def some(n, carry):
            sums = [list(carry[:count]), list(carry[count:])]
            do(low + many * n, sums)
            return tuple(sums[0] + sums[1])

        total = lax.fori_loop(0, (high - low) // many, some, (zero,) * (2 * count))
        return [list(total[:count]), list(total[count:])]

    def inject(field, edges, low, high):
        for q in range(low, high):
            x = at(field, q, 64)
            ghost = jnp.where(low_half, pltpu.roll(x, 65, axis=1), pltpu.roll(x, 64, axis=1))
            put(field, q, 0, jnp.where(lane == 0, pltpu.roll(edges[0], (128 - q) % 128, axis=1), ghost))
            x = at(field, q, 8)
            ghost = jnp.where(low_half, pltpu.roll(x, 64, axis=1), pltpu.roll(x, 63, axis=1))
            put(field, q, 72, jnp.where(lane == 127, pltpu.roll(edges[1], 127 - q, axis=1), ghost))

    def inject_halo(field, edges, near_=0, far_=DEEP):
        inject(field, edges, TOP - far_, TOP - near_)
        inject(field, edges, BOTTOM + near_, BOTTOM + far_)

    def hop(peers, src, got, send, recv, size, mine, u):
        for m, (_, device) in enumerate(peers):
            remote(src.at[u], got.at[u, :, pl.ds(mine, 1), :], send.at[size * u + m], recv.at[size * u + mine], device).start()

    def hop_done(peers, src, got, send, recv, size, u):
        for m, (slot, device) in enumerate(peers):
            remote(src.at[u], got.at[u, :, pl.ds(slot, 1), :], send.at[size * u + m], recv.at[size * u + slot], device).wait()

    def hop1(u, row):
        src1[u, 0] = row
        hop(peers1, src1, got1, s1, r1, near, me1, u)

    def hop1_in(u, row):
        hop_done(peers1, src1, got1, s1, r1, near, u)
        return jnp.where(sublane[0:near] == me1, row, got1[u, 0])

    def hop2(u, rows):
        for h in range(2):
            src2[u, h] = rows[h]
        hop(peers2, src2, got2, s2, r2, chips, chip, u)

    def hop2_in(u, rows):
        hop_done(peers2, src2, got2, s2, r2, chips, u)
        which = lax.broadcasted_iota(jnp.int32, (chips, 128), 0)
        return [jnp.where(which == chip, rows[h], got2[u, h]) for h in range(2)]

    def added(terms):
        while len(terms) > 1:
            terms = [a + b for a, b in zip(terms[::2], terms[1::2])] + terms[len(terms) // 2 * 2 :]
        return terms[0]

    def over_sublanes(v):
        for n in (4, 2, 1):
            v = v + pltpu.roll(v, n, axis=0)
        return v

    def moments_out(u, sums):
        message = zero
        for n, v in enumerate(sums):
            message = jnp.where(sublane == n, over_sublanes(v), message)
        flat = jnp.sum(message, axis=1, keepdims=True)
        row = over_sublanes(jnp.where(lane == sublane, flat, 0.0))[0:1]
        hop1(u, row)
        return row

    def moments_on(u, row):
        row = over_sublanes(hop1_in(u, row))[0:1]
        hop2(u, [row, row])
        return row

    def moments_in(u, row):
        total = over_sublanes(added([v for v in jnp.split(hop2_in(u, [row, row])[0], chips // 8)]))
        return [jnp.broadcast_to(total[:, n : n + 1], (8, 128)) for n in range(6)]

    def solve(moments, sigma):
        g00, g01, g11, g12, g22, h22 = moments
        inverse = 1.0 / sigma
        t0, t1 = SHIFTS
        g02 = g11 + (sigma * (t0 - t1)) * g01
        a00 = inverse * g01 + t0 * g00
        a01 = inverse * g11 + t0 * g01
        a02 = inverse * g12 + t0 * g02
        a11 = inverse * g12 + t1 * g11
        a12 = inverse * g22 + t1 * g12
        a22 = inverse * h22
        i0 = 1.0 / a00
        l10, l20 = a01 * i0, a02 * i0
        d1, u12 = a11 - l10 * a01, a12 - l10 * a02
        i1 = jnp.where(d1 > TINY * a11, 1.0 / d1, 0.0)
        l21 = u12 * i1
        d2 = a22 - l20 * a02 - l21 * u12
        i2 = jnp.where(d2 > TINY * a22, 1.0 / d2, 0.0)
        y0 = 10.0 * g00
        y1 = 10.0 * g01 - l10 * y0
        y2 = 10.0 * g02 - l20 * y0 - l21 * y1
        c2 = y2 * i2
        c1 = y1 * i1 - l21 * c2
        c0 = y0 * i0 - l10 * c1 - l20 * c2
        return c0, c1, c2

    relayout(order[0])
    relayout(order[1])
    for i in (1, 2):
        for n in range(3):
            loads[i, n].wait()
    pack_inputs()
    pl.semaphore_wait(barrier, len(greeted))
    rims = edge_copies(0) + edge_copies(1) + edge_copies(2)
    start(rims)
    halo = row_copies(r_m, 0, 0, 5) + row_copies(kap_m, 2, 0, 4) + row_copies(off_m, 1, 0, 3)
    start(halo)
    rest = row_copies(off_m, 6, 3, 5) + row_copies(kap_m, 5, 4, 6)
    start(rest)
    load_labels.wait()

    def label_copy(k, arriving):
        z = lax.rem(sub + k, subs)
        held = z if arriving else sub
        return remote(labels_h, lab.at[held], lab_s.at[k], lab_r.at[held], (strip, z))

    for k in range(1, subs):
        label_copy(k, False).start()
    relayout(order[2], False)
    relayout(order[3], False)
    alive = (left_open, right_open)
    arrived(rims)
    e_off = [landed(0, to) for to in range(2)]
    e_r = [landed(1, to) * alive[to] for to in range(2)]
    e_kap = [landed(2, to) + 4.0 for to in range(2)]
    e_w = [10.0 * jnp.exp(v) for v in e_off]
    for field, edges in ((kap_m, e_kap), (w_m, e_w), (r_m, e_r)):
        inject(field, edges, TOP, BOTTOM)

    def of_a(r, a):
        return r * r, r * a, a * a

    def of_b(a, b):
        return a * b, b * b

    def closed(sums):
        return [x + y for x, y in zip(*sums)]

    def a_block(q, many, n, sums, counted):
        shift_block(r_m, a_m, q, many, SHIFTS[0], SIGMA[n], of_a, sums, counted)

    def b_block(q, many, n, sums, counted):
        shift_block(a_m, b_m, q, many, SHIFTS[1], SIGMA[n], of_b, sums, counted)

    apply_k(r_m, t_m, 9, 39, 6)
    sums_a = sum_blocks(10, 38, 4, 3, lambda q, sums: a_block(q, 4, 0, sums, range(4)))
    a_rows = row_copies(a_m, 3, 3, 5)
    apply_k(a_m, t_m, 11, 35, 4)
    k_block(a_m, t_m, 35, 2)
    sums_b = sum_blocks(12, 36, 4, 2, lambda q, sums: b_block(q, 4, 0, sums, range(4)))
    sums_e = sum_blocks(13, 33, 4, 1, lambda q, sums: energy_block(q, 4, 1.0, sums))
    energy_block(33, 2, 1.0, sums_e)
    inject(off_m, e_off, TOP, BOTTOM)
    arrived(halo)
    start(a_rows)
    for q in (5, 6, 7, 40, 41, 42):
        for p in OWN:
            put(w_m, q, p, 10.0 * jnp.exp(at(off_m, q, p)))
    inject_halo(kap_m, e_kap, 0, 4)
    inject_halo(w_m, e_w)
    inject_halo(r_m, e_r)
    blank(r_m, TOP - DEEP, BOTTOM + DEEP)
    k_block(r_m, t_m, 4, 5)
    k_block(r_m, t_m, 39, 5)
    blank(t_m, 4, 44)
    a_block(5, 5, 0, sums_a, (3, 4))
    a_block(38, 5, 0, sums_a, (0, 1))
    blank(a_m, 5, 43)
    k_block(a_m, t_m, 6, 5)
    k_block(a_m, t_m, 37, 5)
    blank(t_m, 6, 42)
    b_block(7, 5, 0, sums_b, (1, 2, 3, 4))
    b_block(36, 5, 0, sums_b, (0, 1, 2, 3))
    blank(b_m, 7, 41)
    b_rows = row_copies(b_m, 4, 1, 7)
    start(b_rows)
    energy_block(8, 5, 1.0, sums_e)
    energy_block(35, 5, 1.0, sums_e)
    row0 = moments_out(0, closed(sums_a) + closed(sums_b) + closed(sums_e))
    pack_field(a_m, 3)
    pack_field(b_m, 4)
    ab_rims = edge_copies(3) + edge_copies(4)
    start(ab_rims)
    moving = a_rows + b_rows + ab_rims
    arrived(rest)
    inject_halo(off_m, e_off)
    inject_halo(kap_m, e_kap, 4, 6)
    row0 = moments_on(0, row0)

    arrived(ab_rims)
    inject(a_m, [landed(3, to) for to in range(2)], TOP, BOTTOM)
    e_b = [landed(4, to) * alive[to] for to in range(2)]
    inject(b_m, e_b, TOP, BOTTOM)
    arrived(a_rows)
    inject_halo(a_m, [landed(3, to) for to in range(2)])
    arrived(b_rows)
    inject_halo(b_m, e_b, 0, 7)
    blank(b_m, 1, 47)
    apply_k(b_m, t_m, 2, 46, 4)
    blank(t_m, 2, 46)

    def second_k(q, many):
        for p in ALL:
            made, _ = k_tile(t_m, q, p, many)
            for m in range(many):
                put(q_m, q + m, p, made[m])

    blocks(3, 45, 6, lambda q: second_k(q, 6))
    sent(moving)
    sent(halo)

    c0, c1, c2 = solve(moments_in(0, row0), SIGMA[0])
    d0, d1, d2 = 0.1 * c0, 0.1 * c1, 0.1 * c2

    def renew(off, weight, r, a, b, qb):
        step = c0 * r + (c1 * a + c2 * b)
        q_mode = d0 * (a + (SHIFTS[0] - weight) * r) + (d1 * (b + (SHIFTS[1] - weight) * a) + d2 * qb)
        fresh = jnp.exp(off + step)
        return step, (10.0 * SIGMA[1]) * fresh, ((r + 0.1 * weight) - fresh) - q_mode

    def renew_rows(q, many, keep):
        for p in range(0, PITCH, 8):
            for m in range(many):
                off = at(off_m, q + m, p)
                weight = at(w_m, q + m, p) if keep else 10.0 * jnp.exp(off)
                step, fresh, gradient = renew(off, weight, *(at(f, q + m, p) for f in (r_m, a_m, b_m, q_m)))
                if p == 0:
                    gradient = jnp.where(lane == 0, jnp.where(sub > 0, gradient, 0.0), gradient)
                elif p == 72:
                    gradient = jnp.where(lane == 127, jnp.where(sub < subs - 1, gradient, 0.0), gradient)
                elif keep:
                    put(mode_m, q + m, p, step)
                put(w_m, q + m, p, fresh)
                put(r_m, q + m, p, gradient)

    blocks(TOP, BOTTOM, 2, lambda q: renew_rows(q, 2, True))
    each(TOP - DEEP, TOP, lambda q: renew_rows(q, 1, False))
    each(BOTTOM, BOTTOM + DEEP, lambda q: renew_rows(q, 1, False))
    blank(r_m, TOP - DEEP, BOTTOM + DEEP)

    apply_k(r_m, t_m, 4, 44, 4)
    blank(t_m, 4, 44)
    sums_a = sum_blocks(8, 40, 4, 3, lambda q, sums: a_block(q, 4, 1, sums, range(4)))
    a_block(5, 3, 1, None, ())
    a_block(40, 3, 1, None, ())
    blank(a_m, 5, 43)
    apply_k(a_m, t_m, 6, 42, 4)
    blank(t_m, 6, 42)
    sums_b = sum_blocks(8, 40, 4, 2, lambda q, sums: b_block(q, 4, 1, sums, range(4)))
    b_block(7, 1, 1, None, ())
    b_block(40, 1, 1, None, ())
    blank(b_m, 7, 41)
    sums_e = sum_blocks(8, 40, 4, 1, lambda q, sums: energy_block(q, 4, SIGMA[1], sums))
    row1 = moments_out(1, closed(sums_a) + closed(sums_b) + closed(sums_e))
    row1 = moments_on(1, row1)

    sent(rims)
    sent(rest)
    for k in range(1, subs):
        label_copy(k, True).wait()
    load_owner.wait()
    myself = strip * subs + sub
    mark = jnp.where(own[...] == myself, 1, 0)
    count = mark
    for n in (1, 2, 4, 8, 16, 32, 64):
        count = count + jnp.where(lane >= n, pltpu.roll(count, n, axis=1), 0)
    whole = jnp.broadcast_to(count[:, 127:128], (8, 128))
    below = jnp.where(sublane >= 1, pltpu.roll(whole, 1, axis=0), 0)
    for n in (1, 2, 4):
        below = below + jnp.where(sublane >= n, pltpu.roll(below, n, axis=0), 0)
    slot = jnp.where(mark == 1, count + below - 1, -1)
    region = (sublane * 128 + lane).astype(F32)
    tiles = []
    for h in range(2):
        pair = jnp.concatenate([lab[2 * h], lab[2 * h + 1]], axis=1).astype(F32)
        twice = [jnp.broadcast_to(pair[n : n + 1], (2, 128)) for n in range(8)]
        tiles.append(jnp.concatenate(twice, axis=0))
    for s in range(OWNED_MOST):
        mine = jnp.max(jnp.where(slot == s, region, -1.0), axis=1, keepdims=True)
        mine = jnp.max(mine, axis=0, keepdims=True)
        for h in range(2):
            pick[s, h] = jnp.where(tiles[h] == mine, 1.0, 0.0)

    c0, c1, c2 = solve(moments_in(1, row1), SIGMA[1])

    def finish(q, sums):
        for p in OWN:
            for m in range(2):
                mode = at(mode_m, q + m, p) + (
                    c0 * at(r_m, q + m, p) + (c1 * at(a_m, q + m, p) + c2 * at(b_m, q + m, p))
                )
                put(mode_m, q + m, p, mode)
                summed(sums, m, [jnp.exp(at(off_m, q + m, p) + mode)])

    line = over_sublanes(closed(sum_blocks(TOP, BOTTOM, 2, 1, finish))[0])
    line = line + pltpu.roll(line, 64, axis=1)
    mine = lax.div(lane, 64) == lax.rem(sub, 2)
    row2 = jnp.where(mine, line * (1.0 / (TILE * TILE)), 0.0)[0:1]
    hop1(2, row2)

    outs = []

    def write_out(i):
        def pair(m):
            row = 2 * m
            q = TOP + 8 * i + row
            x = jnp.concatenate([mode_m[q, 8:72, :], mode_m[q + 1, 8:72, :]], axis=0).T
            for g in range(8):
                upper, lower = x[8 * g : 8 * g + 8], x[64 + 8 * g : 72 + 8 * g]
                to = 512 * i + 64 * g + row
                st_o[pl.ds(to, 8, stride=8), :] = jnp.where(low_half, upper, pltpu.roll(lower, 64, axis=1))
                st_o[pl.ds(to + 1, 8, stride=8), :] = jnp.where(low_half, pltpu.roll(upper, 64, axis=1), lower)

        each(0, 4, pair)
        part = pl.ds(512 * i, 512)
        outs.append(pltpu.make_async_copy(st_o.at[part, :], mode_h.at[part, :], out_sem.at[i]))
        outs[-1].start()

    write_out(0)
    write_out(1)
    got = hop1_in(2, row2)
    upper = lax.div(lax.rem(sublane, subs), 2)
    rows2 = [over_sublanes(jnp.where(upper == h, got, 0.0))[0:1] for h in range(2)]
    hop2(2, rows2)
    write_out(2)
    write_out(3)
    total = hop2_in(2, rows2)
    answer = zero
    for h in range(2):
        gathered = zero
        for s in range(8 * h, min(8 * h + 8, OWNED_MOST)):
            both = total[0] * pick[s, 0] + total[1] * pick[s, 1]
            gathered = jnp.where(
                sublane == s - 8 * h, over_sublanes(both[0:8] + both[8:16]), gathered
            )
        flat = jnp.sum(gathered, axis=1, keepdims=True)
        answer = answer + jnp.where(lane == sublane + 8 * h, flat, 0.0)
    owned_ref[...] = over_sublanes(answer)[0:1, 0:OWNED_MOST]
    for copy in outs:
        copy.wait()


def solution(mesh):
    strips, subs = mesh.shape["strip"], mesh.shape["sub"]
    near, chips = 2 * subs, strips // 2

    def tiled(x):
        return x.reshape(4, 8, 64, 128).transpose(0, 2, 1, 3).reshape(2048, 128)

    def body(counts, offset, kappa, labels, owner):
        field = pltpu.VMEM((SLOTS, PITCH, 128), F32)
        stage = pltpu.VMEM((2048, 128), F32)
        dma = pltpu.SemaphoreType.DMA
        anywhere = pl.BlockSpec(memory_space=pl.ANY)
        mode, owned = pl.pallas_call(
            lambda *refs: kernel((strips, subs), *refs),
            out_shape=(
                jax.ShapeDtypeStruct((2048, 128), F32),
                jax.ShapeDtypeStruct((1, OWNED_MOST), F32),
            ),
            in_specs=[anywhere] * 5,
            out_specs=(anywhere, pl.BlockSpec(memory_space=pltpu.VMEM)),
            scratch_shapes=[
                pltpu.VMEM((2048, 128), jnp.int32), stage, stage,
                field, field, field, field, field, field, field, field, field,
                pltpu.VMEM((6, 2, 8, 128), F32),
                pltpu.VMEM((36, 8, 128), F32),
                pltpu.VMEM((subs, 8, labels.shape[1]), jnp.int32),
                pltpu.VMEM((8, 128), jnp.int32),
                pltpu.VMEM((OWNED_MOST, 2, chips, 128), F32),
                pltpu.VMEM((3, 1, 1, 128), F32),
                pltpu.VMEM((3, 2, 1, 128), F32),
                pltpu.VMEM((3, 1, near, 128), F32),
                pltpu.VMEM((3, 2, chips, 128), F32),
                dma((12,)), dma((2,)), dma((14,)), dma((14,)), dma((36,)), dma((36,)),
                dma((subs,)), dma((subs,)), dma((3 * near,)), dma((3 * near,)),
                dma((3 * chips,)), dma((3 * chips,)), dma((4,)),
            ],
            compiler_params=pltpu.CompilerParams(
                collective_id=0, has_side_effects=True, vmem_limit_bytes=63 << 20
            ),
        )(tiled(counts), tiled(offset), tiled(kappa), labels, owner.reshape(8, 128))
        mode = mode.reshape(4, 64, 8, 128).transpose(0, 2, 1, 3).reshape(32, 8192)
        return mode, owned.reshape(OWNED_MOST)

    return jax.shard_map(
        body,
        mesh=mesh,
        in_specs=(P("strip", "sub"), P("strip", "sub"), P("strip", "sub"), P(None, "sub"), P()),
        out_specs=(P("strip", "sub"), P(("strip", "sub"))),
        check_vma=False,
    )
```

```python
import jax
import jax.numpy as jnp
from jax import lax
from jax.experimental import pallas as pl
from jax.experimental.pallas import tpu as pltpu
from jax.sharding import PartitionSpec as P

TILE = 128
OWNED_MOST = 15
MESH = pl.DeviceIdType.MESH
F32 = jnp.float32

ROWS, TOP, BOTTOM, SLOTS, DEEP = 32, 8, 40, 48, 5
PITCH = 80
OWN = tuple(range(8, 72, 8))
ALL = (1,) + OWN + (71,)
SHIFTS = (3.0, 40.0)
SIGMA = (1.0, 2.0**-27)
TINY = 3e-7


def kernel(
    dims, counts_h, offset_h, kappa_h, labels_h, owner_h, mode_h, owned_ref,
    st_c, st_o, st_k, off_m, kap_m, w_m, r_m, t_m, a_m, b_m, q_m, mode_m,
    pack, land, lab, own, pick, src, got,
    ld_sem, small_sem, row_s, row_r, edge_s, edge_r, lab_s, lab_r, sum_s, sum_r, out_sem,
):
    strips, subs = dims
    strip, sub = lax.axis_index("strip"), lax.axis_index("sub")
    core, chip = lax.rem(strip, 2), lax.div(strip, 2)
    devices = strips * subs
    me = sub * strips + strip
    up, down = lax.rem(strip + strips - 1, strips), lax.rem(strip + 1, strips)
    left, right = lax.rem(sub + subs - 1, subs), lax.rem(sub + 1, subs)
    first, last = strip == 0, strip == strips - 1

    side = 4 if strips == 32 else 2
    tall = strips // 2 // side

    def far(n, size):
        return min(n, size - n)

    def turned_by(x, n, size):
        return lax.rem(x + n, size) if n else x

    at_y = [turned_by(lax.div(chip, side), n, tall) for n in range(tall)]
    at_x = [turned_by(lax.rem(chip, side), n, side) for n in range(side)]
    at_z = [turned_by(sub, n, subs) for n in range(subs)]
    peers = []
    for dy, dx, dz, flip in sorted(
        (
            (y, x, z, f) for y in range(tall) for x in range(side) for z in range(subs)
            for f in range(2) if y or x or z or f
        ),
        key=lambda v: -far(v[0], tall) - far(v[1], side) - far(v[2], subs),
    ):
        core_ = 1 - core if flip else core
        peers.append(((at_y[dy] * side + at_x[dx]) * 2 + core_, at_z[dz]))

    def each(low, high, do):
        def step(k, carry):
            do(k)
            return carry

        lax.fori_loop(low, high, step, 0)

    barrier = pltpu.get_barrier_semaphore()
    for device in peers:
        pl.semaphore_signal(barrier, inc=1, device_id=device, device_id_type=MESH)

    order = (0, 3, 1, 2)
    loads = {}
    for i in order:
        for n, (hbm, stage) in enumerate(((offset_h, st_o), (counts_h, st_c), (kappa_h, st_k))):
            part = pl.ds(512 * i, 512)
            loads[i, n] = pltpu.make_async_copy(hbm.at[part, :], stage.at[part, :], ld_sem.at[3 * i + n])
            loads[i, n].start()
    load_owner = pltpu.make_async_copy(owner_h, own, small_sem.at[0])
    load_owner.start()
    load_labels = pltpu.make_async_copy(labels_h, lab.at[sub], small_sem.at[1])
    load_labels.start()

    lane = lax.broadcasted_iota(jnp.int32, (8, 128), 1)
    sublane = lax.broadcasted_iota(jnp.int32, (8, 128), 0)
    low_half = lane < 64
    zero = jnp.zeros((8, 128), F32)

    def relayout(i, wait=True):
        for n in range(3 if wait else 0):
            loads[i, n].wait()

        def pair(m):
            row = 2 * m

            def turned(stage):
                x = [
                    [
                        stage[pl.ds(512 * i + 64 * g + row + d, 8, stride=8), :].astype(F32)
                        for g in range(8)
                    ]
                    for d in range(2)
                ]
                upper = [jnp.where(low_half, x[0][g], pltpu.roll(x[1][g], 64, axis=1)) for g in range(8)]
                lower = [jnp.where(low_half, pltpu.roll(x[0][g], 64, axis=1), x[1][g]) for g in range(8)]
                return jnp.concatenate(upper + lower, axis=0).T

            off, cnt, kap = turned(st_o), turned(st_c), turned(st_k)
            for d in range(2):
                q = TOP + 8 * i + row + d
                part = slice(64 * d, 64 * d + 64)
                weight = jnp.exp(off[part])
                off_m[q, 8:72, :] = off[part]
                kap_m[q, 8:72, :] = kap[part] + 4.0
                w_m[q, 8:72, :] = 10.0 * weight
                r_m[q, 8:72, :] = cnt[part] - weight

        each(0, 4, pair)

    def remote(src, dst, send, recv, device):
        return pltpu.make_async_remote_copy(
            src_ref=src, dst_ref=dst, send_sem=send, recv_sem=recv,
            device_id=device, device_id_type=MESH,
        )

    def row_copies(field, n, low, high):
        many = high - low

        def rows(q):
            return field.at[pl.ds(q, many), pl.ds(8, 64), :]

        return [
            remote(rows(TOP + low), rows(BOTTOM + low), row_s.at[2 * n], row_r.at[2 * n], (up, sub)),
            remote(
                rows(BOTTOM - high), rows(TOP - high),
                row_s.at[2 * n + 1], row_r.at[2 * n + 1], (down, sub),
            ),
        ]

    def edge_copies(n):
        made = []
        for to, beside in ((1, left), (0, right)):
            for m, device in enumerate(((strip, beside), (down, beside), (up, beside))):
                k = 6 * n + 3 * to + m
                made.append(
                    remote(pack.at[n, to], land.at[k], edge_s.at[k], edge_r.at[k], device)
                )
        return made

    def pack_field(field, n):
        tiles = [zero, zero]
        for q in range(TOP, BOTTOM):
            for to, p, l in ((1, 8, 0), (0, 64, 127)):
                moved = pltpu.roll(field[q, p : p + 8, :], (q - l) % 128, axis=1)
                tiles[to] = jnp.where(lane == q, moved, tiles[to])
        for to in range(2):
            pack[n, to] = tiles[to]

    def pack_inputs():
        for to, g, keep in ((1, 0, slice(0, 8)), (0, 63, slice(120, 128))):
            tiles = []
            for stage in (st_o, st_c, st_k):
                x = [stage[pl.ds(512 * i + 8 * g, 8), :].astype(F32) for i in range(4)]
                tiles.append(jnp.concatenate([zero] + x + [zero] * 11, axis=0).T[keep])
            pack[0, to] = tiles[0]
            pack[1, to] = tiles[1] - jnp.exp(tiles[0])
            pack[2, to] = tiles[2]

    def landed(n, to):
        k = 6 * n + 3 * to
        return jnp.where(
            lane < TOP, pltpu.roll(land[k + 1], 96, axis=1),
            jnp.where(lane < BOTTOM, land[k], pltpu.roll(land[k + 2], 32, axis=1)),
        )

    def start(copies):
        for copy in copies:
            copy.start()

    def arrived(copies):
        for copy in copies:
            copy.wait_recv()

    def sent(copies):
        for copy in copies:
            copy.wait_send()

    left_open = jnp.where(sub > 0, 1.0, 0.0).astype(F32)
    right_open = jnp.where(sub < subs - 1, 1.0, 0.0).astype(F32)
    left_shut = jnp.where((lane == 0) & (sublane < 7), 1.0 - left_open, 0.0) > 0.5
    right_shut = jnp.where((lane == 127) & (sublane >= 1), 1.0 - right_open, 0.0) > 0.5

    def at(field, q, p):
        return field[q, p : p + 8, :]

    def put(field, q, p, value):
        field[q, p : p + 8, :] = value

    def k_tile(field, q, p, many):
        window = [at(field, q - 1 + m, p) for m in range(many + 2)]
        made = []
        for m in range(many):
            beside = at(field, q + m, p - 1) + at(field, q + m, p + 1)
            value = at(kap_m, q + m, p) * window[m + 1] - ((window[m] + window[m + 2]) + beside)
            if p == ALL[0]:
                value = jnp.where(left_shut, 0.0, value)
            if p == ALL[-1]:
                value = jnp.where(right_shut, 0.0, value)
            made.append(value)
        return made, window[1:-1]

    def blank(field, low, high):
        nothing = jnp.zeros((PITCH, 128), F32)

        @pl.when(first)
        def _():
            for q in range(low, TOP):
                field[q] = nothing

        @pl.when(last)
        def _():
            for q in range(BOTTOM, high):
                field[q] = nothing

    def blocks(low, high, many, do):
        each(0, (high - low) // many, lambda n: do(low + many * n))

    def k_block(field, out, q, many):
        for p in ALL:
            made, _ = k_tile(field, q, p, many)
            for m in range(many):
                put(out, q + m, p, made[m])

    def apply_k(field, out, low, high, many):
        blocks(low, high, many, lambda q: k_block(field, out, q, many))

    def summed(sums, n, terms):
        sums[n % 2] = [x + y for x, y in zip(sums[n % 2], terms)]

    def shift_block(base, out, q, many, shift, sigma, products, sums, counted):
        for p in ALL:
            made, _ = k_tile(t_m, q, p, many)
            for m in range(many):
                value, weight = at(base, q + m, p), at(w_m, q + m, p)
                got = (made[m] if sigma == 1.0 else sigma * made[m]) + (weight - sigma * shift) * value
                put(out, q + m, p, got)
                if m in counted and p in OWN:
                    summed(sums, m + p // 8, products(value, got))

    def energy_block(q, many, sigma, sums):
        for p in OWN:
            made, values = k_tile(b_m, q, p, many)
            for m in range(many):
                square = made[m] * made[m]
                square = square if sigma == 1.0 else sigma * square
                summed(sums, m + p // 8, [square + at(w_m, q + m, p) * (values[m] * values[m])])

    def sum_blocks(low, high, many, count, do):
        def some(n, carry):
            sums = [list(carry[:count]), list(carry[count:])]
            do(low + many * n, sums)
            return tuple(sums[0] + sums[1])

        total = lax.fori_loop(0, (high - low) // many, some, (zero,) * (2 * count))
        return [list(total[:count]), list(total[count:])]

    def inject(field, edges, low, high):
        for q in range(low, high):
            x = at(field, q, 64)
            ghost = jnp.where(low_half, pltpu.roll(x, 65, axis=1), pltpu.roll(x, 64, axis=1))
            put(field, q, 0, jnp.where(lane == 0, pltpu.roll(edges[0], (128 - q) % 128, axis=1), ghost))
            x = at(field, q, 8)
            ghost = jnp.where(low_half, pltpu.roll(x, 64, axis=1), pltpu.roll(x, 63, axis=1))
            put(field, q, 72, jnp.where(lane == 127, pltpu.roll(edges[1], 127 - q, axis=1), ghost))

    def inject_halo(field, edges, near_=0, far_=DEEP):
        inject(field, edges, TOP - far_, TOP - near_)
        inject(field, edges, BOTTOM + near_, BOTTOM + far_)

    def tell(u, row):
        src[u] = row
        for device in peers:
            remote(src.at[u], got.at[u, pl.ds(me, 1), :], sum_s.at[u], sum_r.at[u], device).start()

    def heard(u, row):
        rows = got.at[u, pl.ds(0, devices - 1), :]
        remote(rows, rows, sum_s.at[u], sum_r.at[u], peers[0]).wait()
        made = []
        for n in range(devices // 8):
            made.append(jnp.where(sublane + 8 * n == me, row, got[u, pl.ds(8 * n, 8), :]))
        return made

    def added(terms):
        while len(terms) > 1:
            terms = [a + b for a, b in zip(terms[::2], terms[1::2])] + terms[len(terms) // 2 * 2 :]
        return terms[0]

    def over_sublanes(v):
        for n in (4, 2, 1):
            v = v + pltpu.roll(v, n, axis=0)
        return v

    def moments_out(u, sums):
        message = zero
        for n, v in enumerate(sums):
            message = jnp.where(sublane == n, over_sublanes(v), message)
        flat = jnp.sum(message, axis=1, keepdims=True)
        row = over_sublanes(jnp.where(lane == sublane, flat, 0.0))[0:1]
        tell(u, row)
        return row

    def moments_in(u, row):
        total = over_sublanes(added(heard(u, row)))
        return [jnp.broadcast_to(total[:, n : n + 1], (8, 128)) for n in range(6)]

    def solve(moments, sigma):
        g00, g01, g11, g12, g22, h22 = moments
        inverse = 1.0 / sigma
        t0, t1 = SHIFTS
        g02 = g11 + (sigma * (t0 - t1)) * g01
        a00 = inverse * g01 + t0 * g00
        a01 = inverse * g11 + t0 * g01
        a02 = inverse * g12 + t0 * g02
        a11 = inverse * g12 + t1 * g11
        a12 = inverse * g22 + t1 * g12
        a22 = inverse * h22
        i0 = 1.0 / a00
        l10, l20 = a01 * i0, a02 * i0
        d1, u12 = a11 - l10 * a01, a12 - l10 * a02
        i1 = jnp.where(d1 > TINY * a11, 1.0 / d1, 0.0)
        l21 = u12 * i1
        d2 = a22 - l20 * a02 - l21 * u12
        i2 = jnp.where(d2 > TINY * a22, 1.0 / d2, 0.0)
        y0 = 10.0 * g00
        y1 = 10.0 * g01 - l10 * y0
        y2 = 10.0 * g02 - l20 * y0 - l21 * y1
        c2 = y2 * i2
        c1 = y1 * i1 - l21 * c2
        c0 = y0 * i0 - l10 * c1 - l20 * c2
        return c0, c1, c2

    relayout(order[0])
    relayout(order[1])
    for i in (1, 2):
        for n in range(3):
            loads[i, n].wait()
    pack_inputs()
    pl.semaphore_wait(barrier, len(peers))
    rims = edge_copies(0) + edge_copies(1) + edge_copies(2)
    start(rims)
    halo = row_copies(r_m, 0, 0, 5) + row_copies(kap_m, 2, 0, 4) + row_copies(off_m, 1, 0, 3)
    start(halo)
    rest = row_copies(off_m, 6, 3, 5) + row_copies(kap_m, 5, 4, 6)
    start(rest)
    load_labels.wait()

    def label_copy(k, arriving):
        z = lax.rem(sub + k, subs)
        held = z if arriving else sub
        return remote(labels_h, lab.at[held], lab_s.at[k], lab_r.at[held], (strip, z))

    for k in range(1, subs):
        label_copy(k, False).start()
    relayout(order[2], False)
    relayout(order[3], False)
    alive = (left_open, right_open)
    arrived(rims)
    e_off = [landed(0, to) for to in range(2)]
    e_r = [landed(1, to) * alive[to] for to in range(2)]
    e_kap = [landed(2, to) + 4.0 for to in range(2)]
    e_w = [10.0 * jnp.exp(v) for v in e_off]
    for field, edges in ((kap_m, e_kap), (w_m, e_w), (r_m, e_r)):
        inject(field, edges, TOP, BOTTOM)

    def of_a(r, a):
        return r * r, r * a, a * a

    def of_b(a, b):
        return a * b, b * b

    def closed(sums):
        return [x + y for x, y in zip(*sums)]

    def a_block(q, many, n, sums, counted):
        shift_block(r_m, a_m, q, many, SHIFTS[0], SIGMA[n], of_a, sums, counted)

    def b_block(q, many, n, sums, counted):
        shift_block(a_m, b_m, q, many, SHIFTS[1], SIGMA[n], of_b, sums, counted)

    apply_k(r_m, t_m, 9, 39, 6)
    sums_a = sum_blocks(10, 38, 4, 3, lambda q, sums: a_block(q, 4, 0, sums, range(4)))
    a_rows = row_copies(a_m, 3, 3, 5)
    apply_k(a_m, t_m, 11, 35, 4)
    k_block(a_m, t_m, 35, 2)
    sums_b = sum_blocks(12, 36, 4, 2, lambda q, sums: b_block(q, 4, 0, sums, range(4)))
    sums_e = sum_blocks(13, 33, 4, 1, lambda q, sums: energy_block(q, 4, 1.0, sums))
    energy_block(33, 2, 1.0, sums_e)
    inject(off_m, e_off, TOP, BOTTOM)
    arrived(halo)
    start(a_rows)
    for q in (5, 6, 7, 40, 41, 42):
        for p in OWN:
            put(w_m, q, p, 10.0 * jnp.exp(at(off_m, q, p)))
    inject_halo(kap_m, e_kap, 0, 4)
    inject_halo(w_m, e_w)
    inject_halo(r_m, e_r)
    blank(r_m, TOP - DEEP, BOTTOM + DEEP)
    k_block(r_m, t_m, 4, 5)
    k_block(r_m, t_m, 39, 5)
    blank(t_m, 4, 44)
    a_block(5, 5, 0, sums_a, (3, 4))
    a_block(38, 5, 0, sums_a, (0, 1))
    blank(a_m, 5, 43)
    k_block(a_m, t_m, 6, 5)
    k_block(a_m, t_m, 37, 5)
    blank(t_m, 6, 42)
    b_block(7, 5, 0, sums_b, (1, 2, 3, 4))
    b_block(36, 5, 0, sums_b, (0, 1, 2, 3))
    blank(b_m, 7, 41)
    b_rows = row_copies(b_m, 4, 1, 7)
    start(b_rows)
    energy_block(8, 5, 1.0, sums_e)
    energy_block(35, 5, 1.0, sums_e)
    row0 = moments_out(0, closed(sums_a) + closed(sums_b) + closed(sums_e))
    pack_field(a_m, 3)
    pack_field(b_m, 4)
    ab_rims = edge_copies(3) + edge_copies(4)
    start(ab_rims)
    moving = a_rows + b_rows + ab_rims
    arrived(rest)
    inject_halo(off_m, e_off)
    inject_halo(kap_m, e_kap, 4, 6)

    arrived(ab_rims)
    inject(a_m, [landed(3, to) for to in range(2)], TOP, BOTTOM)
    e_b = [landed(4, to) * alive[to] for to in range(2)]
    inject(b_m, e_b, TOP, BOTTOM)
    arrived(a_rows)
    inject_halo(a_m, [landed(3, to) for to in range(2)])
    arrived(b_rows)
    inject_halo(b_m, e_b, 0, 7)
    blank(b_m, 1, 47)
    apply_k(b_m, t_m, 2, 46, 4)
    blank(t_m, 2, 46)

    def second_k(q, many):
        for p in ALL:
            made, _ = k_tile(t_m, q, p, many)
            for m in range(many):
                put(q_m, q + m, p, made[m])

    blocks(3, 45, 6, lambda q: second_k(q, 6))
    sent(moving)
    sent(halo)

    c0, c1, c2 = solve(moments_in(0, row0), SIGMA[0])
    d0, d1, d2 = 0.1 * c0, 0.1 * c1, 0.1 * c2

    def renew(off, weight, r, a, b, qb):
        step = c0 * r + (c1 * a + c2 * b)
        q_mode = d0 * (a + (SHIFTS[0] - weight) * r) + (d1 * (b + (SHIFTS[1] - weight) * a) + d2 * qb)
        fresh = jnp.exp(off + step)
        return step, (10.0 * SIGMA[1]) * fresh, ((r + 0.1 * weight) - fresh) - q_mode

    def renew_rows(q, many, keep):
        for p in range(0, PITCH, 8):
            for m in range(many):
                off = at(off_m, q + m, p)
                weight = at(w_m, q + m, p) if keep else 10.0 * jnp.exp(off)
                step, fresh, gradient = renew(off, weight, *(at(f, q + m, p) for f in (r_m, a_m, b_m, q_m)))
                if p == 0:
                    gradient = jnp.where(lane == 0, jnp.where(sub > 0, gradient, 0.0), gradient)
                elif p == 72:
                    gradient = jnp.where(lane == 127, jnp.where(sub < subs - 1, gradient, 0.0), gradient)
                elif keep:
                    put(mode_m, q + m, p, step)
                put(w_m, q + m, p, fresh)
                put(r_m, q + m, p, gradient)

    blocks(TOP, BOTTOM, 2, lambda q: renew_rows(q, 2, True))
    each(TOP - DEEP, TOP, lambda q: renew_rows(q, 1, False))
    each(BOTTOM, BOTTOM + DEEP, lambda q: renew_rows(q, 1, False))
    blank(r_m, TOP - DEEP, BOTTOM + DEEP)

    apply_k(r_m, t_m, 4, 44, 4)
    blank(t_m, 4, 44)
    sums_a = sum_blocks(8, 40, 4, 3, lambda q, sums: a_block(q, 4, 1, sums, range(4)))
    a_block(5, 3, 1, None, ())
    a_block(40, 3, 1, None, ())
    blank(a_m, 5, 43)
    apply_k(a_m, t_m, 6, 42, 4)
    blank(t_m, 6, 42)
    sums_b = sum_blocks(8, 40, 4, 2, lambda q, sums: b_block(q, 4, 1, sums, range(4)))
    b_block(7, 1, 1, None, ())
    b_block(40, 1, 1, None, ())
    blank(b_m, 7, 41)
    sums_e = sum_blocks(8, 40, 4, 1, lambda q, sums: energy_block(q, 4, SIGMA[1], sums))
    row1 = moments_out(1, closed(sums_a) + closed(sums_b) + closed(sums_e))

    sent(rims)
    sent(rest)
    for k in range(1, subs):
        label_copy(k, True).wait()
    load_owner.wait()
    myself = strip * subs + sub
    mark = jnp.where(own[...] == myself, 1, 0)
    count = mark
    for n in (1, 2, 4, 8, 16, 32, 64):
        count = count + jnp.where(lane >= n, pltpu.roll(count, n, axis=1), 0)
    whole = jnp.broadcast_to(count[:, 127:128], (8, 128))
    below = jnp.where(sublane >= 1, pltpu.roll(whole, 1, axis=0), 0)
    for n in (1, 2, 4):
        below = below + jnp.where(sublane >= n, pltpu.roll(below, n, axis=0), 0)
    slot = jnp.where(mark == 1, count + below - 1, -1)
    region = (sublane * 128 + lane).astype(F32)
    tiles = []
    for z in range(subs):
        wide = jnp.concatenate([lab[z], jnp.full_like(lab[z], -2)], axis=1).astype(F32)
        for n in range(strips // 8):
            two = [jnp.broadcast_to(wide[2 * n + k : 2 * n + k + 1], (4, 128)) for k in range(2)]
            tiles.append(jnp.concatenate(two, axis=0))
    for s in range(OWNED_MOST):
        mine = jnp.max(jnp.where(slot == s, region, -1.0), axis=1, keepdims=True)
        mine = jnp.max(mine, axis=0, keepdims=True)
        for n in range(devices // 8):
            pick[s, pl.ds(8 * n, 8), :] = jnp.where(tiles[n] == mine, 1.0, 0.0)

    c0, c1, c2 = solve(moments_in(1, row1), SIGMA[1])

    def finish(q, sums):
        for p in OWN:
            for m in range(2):
                mode = at(mode_m, q + m, p) + (
                    c0 * at(r_m, q + m, p) + (c1 * at(a_m, q + m, p) + c2 * at(b_m, q + m, p))
                )
                put(mode_m, q + m, p, mode)
                summed(sums, m, [jnp.exp(at(off_m, q + m, p) + mode)])

    line = over_sublanes(closed(sum_blocks(TOP, BOTTOM, 2, 1, finish))[0])
    line = line + pltpu.roll(line, 64, axis=1)
    row2 = (line * (1.0 / (TILE * TILE)))[0:1]
    tell(2, row2)

    outs = []

    def write_out(i):
        def pair(m):
            row = 2 * m
            q = TOP + 8 * i + row
            x = jnp.concatenate([mode_m[q, 8:72, :], mode_m[q + 1, 8:72, :]], axis=0).T
            for g in range(8):
                upper, lower = x[8 * g : 8 * g + 8], x[64 + 8 * g : 72 + 8 * g]
                to = 512 * i + 64 * g + row
                st_o[pl.ds(to, 8, stride=8), :] = jnp.where(low_half, upper, pltpu.roll(lower, 64, axis=1))
                st_o[pl.ds(to + 1, 8, stride=8), :] = jnp.where(low_half, pltpu.roll(upper, 64, axis=1), lower)

        each(0, 4, pair)
        part = pl.ds(512 * i, 512)
        outs.append(pltpu.make_async_copy(st_o.at[part, :], mode_h.at[part, :], out_sem.at[i]))
        outs[-1].start()

    write_out(0)
    write_out(1)
    write_out(2)
    write_out(3)
    total = heard(2, row2)
    answer = zero
    for h in range(2):
        gathered = zero
        for s in range(8 * h, min(8 * h + 8, OWNED_MOST)):
            both = added([v * pick[s, pl.ds(8 * n, 8), :] for n, v in enumerate(total)])
            gathered = jnp.where(
                sublane == s - 8 * h, over_sublanes(both), gathered
            )
        flat = jnp.sum(gathered, axis=1, keepdims=True)
        answer = answer + jnp.where(lane == sublane + 8 * h, flat, 0.0)
    owned_ref[...] = over_sublanes(answer)[0:1, 0:OWNED_MOST]
    for copy in outs:
        copy.wait()


def solution(mesh):
    strips, subs = mesh.shape["strip"], mesh.shape["sub"]
    devices = strips * subs

    def tiled(x):
        return x.reshape(4, 8, 64, 128).transpose(0, 2, 1, 3).reshape(2048, 128)

    def body(counts, offset, kappa, labels, owner):
        field = pltpu.VMEM((SLOTS, PITCH, 128), F32)
        stage = pltpu.VMEM((2048, 128), F32)
        dma = pltpu.SemaphoreType.DMA
        anywhere = pl.BlockSpec(memory_space=pl.ANY)
        mode, owned = pl.pallas_call(
            lambda *refs: kernel((strips, subs), *refs),
            out_shape=(
                jax.ShapeDtypeStruct((2048, 128), F32),
                jax.ShapeDtypeStruct((1, OWNED_MOST), F32),
            ),
            in_specs=[anywhere] * 5,
            out_specs=(anywhere, pl.BlockSpec(memory_space=pltpu.VMEM)),
            scratch_shapes=[
                pltpu.VMEM((2048, 128), jnp.int32), stage, stage,
                field, field, field, field, field, field, field, field, field,
                pltpu.VMEM((6, 2, 8, 128), F32),
                pltpu.VMEM((36, 8, 128), F32),
                pltpu.VMEM((subs, 8, labels.shape[1]), jnp.int32),
                pltpu.VMEM((8, 128), jnp.int32),
                pltpu.VMEM((OWNED_MOST, devices, 128), F32),
                pltpu.VMEM((3, 1, 128), F32),
                pltpu.VMEM((3, devices, 128), F32),
                dma((12,)), dma((2,)), dma((14,)), dma((14,)), dma((36,)), dma((36,)),
                dma((subs,)), dma((subs,)), dma((3,)), dma((3,)), dma((4,)),
            ],
            compiler_params=pltpu.CompilerParams(
                collective_id=0, has_side_effects=True, vmem_limit_bytes=55000000
            ),
        )(tiled(counts), tiled(offset), tiled(kappa), labels, owner.reshape(8, 128))
        mode = mode.reshape(4, 64, 8, 128).transpose(0, 2, 1, 3).reshape(32, 8192)
        return mode, owned.reshape(OWNED_MOST)

    return jax.shard_map(
        body,
        mesh=mesh,
        in_specs=(P("strip", "sub"), P("strip", "sub"), P("strip", "sub"), P(None, "sub"), P()),
        out_specs=(P("strip", "sub"), P(("strip", "sub"))),
        check_vma=False,
    )
```

```python
import jax
import jax.numpy as jnp
from jax import lax
from jax.experimental import pallas as pl
from jax.experimental.pallas import tpu as pltpu
from jax.sharding import PartitionSpec as P

TILE = 128
OWNED_MOST = 15
MESH = pl.DeviceIdType.MESH
F32 = jnp.float32

ROWS, TOP, BOTTOM, SLOTS, DEEP = 32, 8, 40, 48, 5
PITCH = 80
OWN = tuple(range(8, 72, 8))
ALL = (1,) + OWN + (71,)
SHIFTS = (3.0, 40.0)
SIGMA = (1.0, 2.0**-27)
TINY = 3e-7


def kernel(
    dims, counts_h, offset_h, kappa_h, labels_h, owner_h, mode_h, owned_ref,
    st_c, st_o, st_k, off_m, kap_m, w_m, r_m, t_m, a_m, b_m, q_m, mode_m,
    pack, land, lab, own, pick, src, got,
    ld_sem, small_sem, row_s, row_r, edge_s, edge_r, lab_s, lab_r, sum_s, sum_r, out_sem,
):
    strips, subs = dims
    strip, sub = lax.axis_index("strip"), lax.axis_index("sub")
    core, chip = lax.rem(strip, 2), lax.div(strip, 2)
    devices = strips * subs
    me = sub * strips + strip
    up, down = lax.rem(strip + strips - 1, strips), lax.rem(strip + 1, strips)
    left, right = lax.rem(sub + subs - 1, subs), lax.rem(sub + 1, subs)
    first, last = strip == 0, strip == strips - 1

    side = 4 if strips == 32 else 2
    tall = strips // 2 // side

    def far(n, size):
        return min(n, size - n)

    def turned_by(x, n, size):
        return lax.rem(x + n, size) if n else x

    at_y = [turned_by(lax.div(chip, side), n, tall) for n in range(tall)]
    at_x = [turned_by(lax.rem(chip, side), n, side) for n in range(side)]
    at_z = [turned_by(sub, n, subs) for n in range(subs)]
    peers = []
    for dy, dx, dz, flip in sorted(
        (
            (y, x, z, f) for y in range(tall) for x in range(side) for z in range(subs)
            for f in range(2) if y or x or z or f
        ),
        key=lambda v: -far(v[0], tall) - far(v[1], side) - far(v[2], subs),
    ):
        core_ = 1 - core if flip else core
        peers.append(((at_y[dy] * side + at_x[dx]) * 2 + core_, at_z[dz]))

    def each(low, high, do):
        def step(k, carry):
            do(k)
            return carry

        lax.fori_loop(low, high, step, 0)

    barrier = pltpu.get_barrier_semaphore()
    for device in peers:
        pl.semaphore_signal(barrier, inc=1, device_id=device, device_id_type=MESH)

    order = (0, 3, 1, 2)
    loads = {}
    for i in order:
        for n, (hbm, stage) in enumerate(((offset_h, st_o), (counts_h, st_c), (kappa_h, st_k))):
            part = pl.ds(512 * i, 512)
            loads[i, n] = pltpu.make_async_copy(hbm.at[part, :], stage.at[part, :], ld_sem.at[3 * i + n])
            loads[i, n].start()
    load_owner = pltpu.make_async_copy(owner_h, own, small_sem.at[0])
    load_owner.start()
    load_labels = pltpu.make_async_copy(labels_h, lab.at[sub], small_sem.at[1])
    load_labels.start()

    lane = lax.broadcasted_iota(jnp.int32, (8, 128), 1)
    sublane = lax.broadcasted_iota(jnp.int32, (8, 128), 0)
    low_half = lane < 64
    zero = jnp.zeros((8, 128), F32)

    def relayout(i, wait=True):
        for n in range(3 if wait else 0):
            loads[i, n].wait()

        def pair(m):
            row = 2 * m

            def turned(stage):
                x = [
                    [
                        stage[pl.ds(512 * i + 64 * g + row + d, 8, stride=8), :].astype(F32)
                        for g in range(8)
                    ]
                    for d in range(2)
                ]
                upper = [jnp.where(low_half, x[0][g], pltpu.roll(x[1][g], 64, axis=1)) for g in range(8)]
                lower = [jnp.where(low_half, pltpu.roll(x[0][g], 64, axis=1), x[1][g]) for g in range(8)]
                return jnp.concatenate(upper + lower, axis=0).T

            off, cnt, kap = turned(st_o), turned(st_c), turned(st_k)
            for d in range(2):
                q = TOP + 8 * i + row + d
                part = slice(64 * d, 64 * d + 64)
                weight = jnp.exp(off[part])
                off_m[q, 8:72, :] = off[part]
                kap_m[q, 8:72, :] = kap[part] + 4.0
                w_m[q, 8:72, :] = 10.0 * weight
                r_m[q, 8:72, :] = cnt[part] - weight

        each(0, 4, pair)

    def remote(src, dst, send, recv, device):
        return pltpu.make_async_remote_copy(
            src_ref=src, dst_ref=dst, send_sem=send, recv_sem=recv,
            device_id=device, device_id_type=MESH,
        )

    def row_copies(field, n, low, high):
        many = high - low

        def rows(q):
            return field.at[pl.ds(q, many), pl.ds(8, 64), :]

        return [
            remote(rows(TOP + low), rows(BOTTOM + low), row_s.at[2 * n], row_r.at[2 * n], (up, sub)),
            remote(
                rows(BOTTOM - high), rows(TOP - high),
                row_s.at[2 * n + 1], row_r.at[2 * n + 1], (down, sub),
            ),
        ]

    def edge_copies(n):
        made = []
        for to, beside in ((1, left), (0, right)):
            for m, device in enumerate(((strip, beside), (down, beside), (up, beside))):
                k = 6 * n + 3 * to + m
                made.append(
                    remote(pack.at[n, to], land.at[k], edge_s.at[k], edge_r.at[k], device)
                )
        return made

    def pack_field(field, n):
        tiles = [zero, zero]
        for q in range(TOP, BOTTOM):
            for to, p, l in ((1, 8, 0), (0, 64, 127)):
                moved = pltpu.roll(field[q, p : p + 8, :], (q - l) % 128, axis=1)
                tiles[to] = jnp.where(lane == q, moved, tiles[to])
        for to in range(2):
            pack[n, to] = tiles[to]

    def pack_inputs():
        for to, g, keep in ((1, 0, slice(0, 8)), (0, 63, slice(120, 128))):
            tiles = []
            for stage in (st_o, st_c, st_k):
                x = [stage[pl.ds(512 * i + 8 * g, 8), :].astype(F32) for i in range(4)]
                tiles.append(jnp.concatenate([zero] + x + [zero] * 11, axis=0).T[keep])
            pack[0, to] = tiles[0]
            pack[1, to] = tiles[1] - jnp.exp(tiles[0])
            pack[2, to] = tiles[2]

    def landed(n, to):
        k = 6 * n + 3 * to
        return jnp.where(
            lane < TOP, pltpu.roll(land[k + 1], 96, axis=1),
            jnp.where(lane < BOTTOM, land[k], pltpu.roll(land[k + 2], 32, axis=1)),
        )

    def start(copies):
        for copy in copies:
            copy.start()

    def arrived(copies):
        for copy in copies:
            copy.wait_recv()

    def sent(copies):
        for copy in copies:
            copy.wait_send()

    left_open = jnp.where(sub > 0, 1.0, 0.0).astype(F32)
    right_open = jnp.where(sub < subs - 1, 1.0, 0.0).astype(F32)
    left_shut = jnp.where((lane == 0) & (sublane < 7), 1.0 - left_open, 0.0) > 0.5
    right_shut = jnp.where((lane == 127) & (sublane >= 1), 1.0 - right_open, 0.0) > 0.5

    def at(field, q, p):
        return field[q, p : p + 8, :]

    def put(field, q, p, value):
        field[q, p : p + 8, :] = value

    def k_tile(field, q, p, many):
        window = [at(field, q - 1 + m, p) for m in range(many + 2)]
        made = []
        for m in range(many):
            beside = at(field, q + m, p - 1) + at(field, q + m, p + 1)
            value = at(kap_m, q + m, p) * window[m + 1] - ((window[m] + window[m + 2]) + beside)
            if p == ALL[0]:
                value = jnp.where(left_shut, 0.0, value)
            if p == ALL[-1]:
                value = jnp.where(right_shut, 0.0, value)
            made.append(value)
        return made, window[1:-1]

    def blank(field, low, high):
        nothing = jnp.zeros((PITCH, 128), F32)

        @pl.when(first)
        def _():
            for q in range(low, TOP):
                field[q] = nothing

        @pl.when(last)
        def _():
            for q in range(BOTTOM, high):
                field[q] = nothing

    def blocks(low, high, many, do):
        each(0, (high - low) // many, lambda n: do(low + many * n))

    def k_block(field, out, q, many, tiles=ALL):
        for p in tiles:
            made, _ = k_tile(field, q, p, many)
            for m in range(many):
                put(out, q + m, p, made[m])

    def apply_k(field, out, low, high, many, tiles=ALL):
        blocks(low, high, many, lambda q: k_block(field, out, q, many, tiles))

    def summed(sums, n, terms):
        sums[n % 2] = [x + y for x, y in zip(sums[n % 2], terms)]

    def shift_block(base, out, q, many, shift, sigma, products, sums, counted):
        for p in ALL:
            made, _ = k_tile(t_m, q, p, many)
            for m in range(many):
                value, weight = at(base, q + m, p), at(w_m, q + m, p)
                got = (made[m] if sigma == 1.0 else sigma * made[m]) + (weight - sigma * shift) * value
                put(out, q + m, p, got)
                if m in counted and p in OWN:
                    summed(sums, m + p // 8, products(value, got))

    def energy_block(q, many, sigma, sums):
        for p in OWN:
            made, values = k_tile(b_m, q, p, many)
            for m in range(many):
                square = made[m] * made[m]
                square = square if sigma == 1.0 else sigma * square
                summed(sums, m + p // 8, [square + at(w_m, q + m, p) * (values[m] * values[m])])

    def sum_blocks(low, high, many, count, do):
        def some(n, carry):
            sums = [list(carry[:count]), list(carry[count:])]
            do(low + many * n, sums)
            return tuple(sums[0] + sums[1])

        total = lax.fori_loop(0, (high - low) // many, some, (zero,) * (2 * count))
        return [list(total[:count]), list(total[count:])]

    def inject(field, edges, low, high):
        for q in range(low, high):
            x = at(field, q, 64)
            ghost = jnp.where(low_half, pltpu.roll(x, 65, axis=1), pltpu.roll(x, 64, axis=1))
            put(field, q, 0, jnp.where(lane == 0, pltpu.roll(edges[0], (128 - q) % 128, axis=1), ghost))
            x = at(field, q, 8)
            ghost = jnp.where(low_half, pltpu.roll(x, 64, axis=1), pltpu.roll(x, 63, axis=1))
            put(field, q, 72, jnp.where(lane == 127, pltpu.roll(edges[1], 127 - q, axis=1), ghost))

    def inject_halo(field, edges, near_=0, far_=DEEP):
        inject(field, edges, TOP - far_, TOP - near_)
        inject(field, edges, BOTTOM + near_, BOTTOM + far_)

    def tell(u, row):
        src[u] = row
        for device in peers:
            remote(src.at[u], got.at[u, pl.ds(me, 1), :], sum_s.at[u], sum_r.at[u], device).start()

    def heard(u, row):
        rows = got.at[u, pl.ds(0, devices - 1), :]
        remote(rows, rows, sum_s.at[u], sum_r.at[u], peers[0]).wait()
        made = []
        for n in range(devices // 8):
            made.append(jnp.where(sublane + 8 * n == me, row, got[u, pl.ds(8 * n, 8), :]))
        return made

    def added(terms):
        while len(terms) > 1:
            terms = [a + b for a, b in zip(terms[::2], terms[1::2])] + terms[len(terms) // 2 * 2 :]
        return terms[0]

    def over_sublanes(v):
        for n in (4, 2, 1):
            v = v + pltpu.roll(v, n, axis=0)
        return v

    def moments_out(u, sums):
        message = zero
        for n, v in enumerate(sums):
            message = jnp.where(sublane == n, over_sublanes(v), message)
        flat = jnp.sum(message, axis=1, keepdims=True)
        row = over_sublanes(jnp.where(lane == sublane, flat, 0.0))[0:1]
        tell(u, row)
        return row

    def moments_in(u, row):
        total = over_sublanes(added(heard(u, row)))
        return [jnp.broadcast_to(total[:, n : n + 1], (8, 128)) for n in range(6)]

    def solve(moments, sigma):
        g00, g01, g11, g12, g22, h22 = moments
        inverse = 1.0 / sigma
        t0, t1 = SHIFTS
        g02 = g11 + (sigma * (t0 - t1)) * g01
        a00 = inverse * g01 + t0 * g00
        a01 = inverse * g11 + t0 * g01
        a02 = inverse * g12 + t0 * g02
        a11 = inverse * g12 + t1 * g11
        a12 = inverse * g22 + t1 * g12
        a22 = inverse * h22
        i0 = 1.0 / a00
        l10, l20 = a01 * i0, a02 * i0
        d1, u12 = a11 - l10 * a01, a12 - l10 * a02
        i1 = jnp.where(d1 > TINY * a11, 1.0 / d1, 0.0)
        l21 = u12 * i1
        d2 = a22 - l20 * a02 - l21 * u12
        i2 = jnp.where(d2 > TINY * a22, 1.0 / d2, 0.0)
        y0 = 10.0 * g00
        y1 = 10.0 * g01 - l10 * y0
        y2 = 10.0 * g02 - l20 * y0 - l21 * y1
        c2 = y2 * i2
        c1 = y1 * i1 - l21 * c2
        c0 = y0 * i0 - l10 * c1 - l20 * c2
        return c0, c1, c2

    relayout(order[0])
    relayout(order[1])
    for i in (1, 2):
        for n in range(3):
            loads[i, n].wait()
    pack_inputs()
    pl.semaphore_wait(barrier, len(peers))
    rims = edge_copies(0) + edge_copies(1) + edge_copies(2)
    start(rims)
    halo = row_copies(r_m, 0, 0, 5) + row_copies(kap_m, 2, 0, 4) + row_copies(off_m, 1, 0, 3)
    start(halo)
    rest = row_copies(off_m, 6, 3, 5) + row_copies(kap_m, 5, 4, 6)
    start(rest)
    load_labels.wait()

    def label_copy(k, arriving):
        z = lax.rem(sub + k, subs)
        held = z if arriving else sub
        return remote(labels_h, lab.at[held], lab_s.at[k], lab_r.at[held], (strip, z))

    for k in range(1, subs):
        label_copy(k, False).start()
    relayout(order[2], False)
    relayout(order[3], False)
    alive = (left_open, right_open)
    arrived(rims)
    e_off = [landed(0, to) for to in range(2)]
    e_r = [landed(1, to) * alive[to] for to in range(2)]
    e_kap = [landed(2, to) + 4.0 for to in range(2)]
    e_w = [10.0 * jnp.exp(v) for v in e_off]
    for field, edges in ((kap_m, e_kap), (w_m, e_w), (r_m, e_r)):
        inject(field, edges, TOP, BOTTOM)

    def of_a(r, a):
        return r * r, r * a, a * a

    def of_b(a, b):
        return a * b, b * b

    def closed(sums):
        return [x + y for x, y in zip(*sums)]

    def a_block(q, many, n, sums, counted):
        shift_block(r_m, a_m, q, many, SHIFTS[0], SIGMA[n], of_a, sums, counted)

    def b_block(q, many, n, sums, counted):
        shift_block(a_m, b_m, q, many, SHIFTS[1], SIGMA[n], of_b, sums, counted)

    apply_k(r_m, t_m, 9, 39, 6)
    sums_a = sum_blocks(10, 38, 4, 3, lambda q, sums: a_block(q, 4, 0, sums, range(4)))
    a_rows = row_copies(a_m, 3, 3, 5)
    start(a_rows)
    apply_k(a_m, t_m, 11, 35, 4)
    k_block(a_m, t_m, 35, 2)
    sums_b = sum_blocks(12, 36, 4, 2, lambda q, sums: b_block(q, 4, 0, sums, range(4)))
    b_rows = row_copies(b_m, 7, 4, 7)
    start(b_rows)
    sums_e = sum_blocks(13, 33, 4, 1, lambda q, sums: energy_block(q, 4, 1.0, sums))
    energy_block(33, 2, 1.0, sums_e)
    inject(off_m, e_off, TOP, BOTTOM)
    arrived(halo)
    for q in (5, 6, 7, 40, 41, 42):
        for p in OWN:
            put(w_m, q, p, 10.0 * jnp.exp(at(off_m, q, p)))
    inject_halo(kap_m, e_kap, 0, 4)
    inject_halo(w_m, e_w)
    inject_halo(r_m, e_r)
    blank(r_m, TOP - DEEP, BOTTOM + DEEP)
    k_block(r_m, t_m, 4, 5)
    k_block(r_m, t_m, 39, 5)
    blank(t_m, 4, 44)
    a_block(5, 5, 0, sums_a, (3, 4))
    a_block(38, 5, 0, sums_a, (0, 1))
    blank(a_m, 5, 43)
    k_block(a_m, t_m, 6, 5)
    k_block(a_m, t_m, 37, 5)
    blank(t_m, 6, 42)
    b_block(7, 5, 0, sums_b, (1, 2, 3, 4))
    b_block(36, 5, 0, sums_b, (0, 1, 2, 3))
    blank(b_m, 7, 41)
    outer = row_copies(b_m, 4, 1, 4)
    start(outer)
    b_rows = b_rows + outer
    energy_block(8, 5, 1.0, sums_e)
    energy_block(35, 5, 1.0, sums_e)
    pack_field(a_m, 3)
    pack_field(b_m, 4)
    ab_rims = edge_copies(3) + edge_copies(4)
    start(ab_rims)
    row0 = moments_out(0, closed(sums_a) + closed(sums_b) + closed(sums_e))
    moving = a_rows + b_rows + ab_rims
    arrived(rest)
    inject_halo(off_m, e_off)
    inject_halo(kap_m, e_kap, 4, 6)

    def second_k(q, many, tiles=ALL):
        for p in tiles:
            made, _ = k_tile(t_m, q, p, many)
            for m in range(many):
                put(q_m, q + m, p, made[m])

    apply_k(b_m, t_m, 9, 39, 6, OWN)
    blocks(10, 38, 4, lambda q: second_k(q, 4, OWN[1:-1]))
    arrived(ab_rims)
    e_b = [landed(4, to) * alive[to] for to in range(2)]
    inject(b_m, e_b, TOP, BOTTOM)
    apply_k(b_m, t_m, 9, 39, 6, ALL[::9])
    blocks(10, 38, 4, lambda q: second_k(q, 4, ALL[:2] + ALL[-2:]))
    inject(a_m, [landed(3, to) for to in range(2)], TOP, BOTTOM)
    arrived(a_rows)
    inject_halo(a_m, [landed(3, to) for to in range(2)])
    arrived(b_rows)
    inject_halo(b_m, e_b, 0, 7)
    blank(b_m, 1, 47)
    for q in (2, 39):
        k_block(b_m, t_m, q, 7)
    blank(t_m, 2, 46)
    for q in (3, 38):
        second_k(q, 7)
    sent(moving)
    sent(halo)

    c0, c1, c2 = solve(moments_in(0, row0), SIGMA[0])
    d0, d1, d2 = 0.1 * c0, 0.1 * c1, 0.1 * c2

    def renew(off, weight, r, a, b, qb):
        step = c0 * r + (c1 * a + c2 * b)
        q_mode = d0 * (a + (SHIFTS[0] - weight) * r) + (d1 * (b + (SHIFTS[1] - weight) * a) + d2 * qb)
        fresh = jnp.exp(off + step)
        return step, (10.0 * SIGMA[1]) * fresh, ((r + 0.1 * weight) - fresh) - q_mode

    def renew_rows(q, many, keep):
        for p in range(0, PITCH, 8):
            for m in range(many):
                off = at(off_m, q + m, p)
                weight = at(w_m, q + m, p) if keep else 10.0 * jnp.exp(off)
                step, fresh, gradient = renew(off, weight, *(at(f, q + m, p) for f in (r_m, a_m, b_m, q_m)))
                if p == 0:
                    gradient = jnp.where(lane == 0, jnp.where(sub > 0, gradient, 0.0), gradient)
                elif p == 72:
                    gradient = jnp.where(lane == 127, jnp.where(sub < subs - 1, gradient, 0.0), gradient)
                elif keep:
                    put(mode_m, q + m, p, step)
                put(w_m, q + m, p, fresh)
                put(r_m, q + m, p, gradient)

    blocks(TOP, BOTTOM, 2, lambda q: renew_rows(q, 2, True))
    each(TOP - DEEP, TOP, lambda q: renew_rows(q, 1, False))
    each(BOTTOM, BOTTOM + DEEP, lambda q: renew_rows(q, 1, False))
    blank(r_m, TOP - DEEP, BOTTOM + DEEP)

    apply_k(r_m, t_m, 4, 44, 4)
    blank(t_m, 4, 44)
    sums_a = sum_blocks(8, 40, 4, 3, lambda q, sums: a_block(q, 4, 1, sums, range(4)))
    a_block(5, 3, 1, None, ())
    a_block(40, 3, 1, None, ())
    blank(a_m, 5, 43)
    apply_k(a_m, t_m, 6, 42, 4)
    blank(t_m, 6, 42)
    sums_b = sum_blocks(8, 40, 4, 2, lambda q, sums: b_block(q, 4, 1, sums, range(4)))
    b_block(7, 1, 1, None, ())
    b_block(40, 1, 1, None, ())
    blank(b_m, 7, 41)
    sums_e = sum_blocks(8, 40, 4, 1, lambda q, sums: energy_block(q, 4, SIGMA[1], sums))
    row1 = moments_out(1, closed(sums_a) + closed(sums_b) + closed(sums_e))

    sent(rims)
    sent(rest)
    for k in range(1, subs):
        label_copy(k, True).wait()
    load_owner.wait()
    myself = strip * subs + sub
    mark = jnp.where(own[...] == myself, 1, 0)
    count = mark
    for n in (1, 2, 4, 8, 16, 32, 64):
        count = count + jnp.where(lane >= n, pltpu.roll(count, n, axis=1), 0)
    whole = jnp.broadcast_to(count[:, 127:128], (8, 128))
    below = jnp.where(sublane >= 1, pltpu.roll(whole, 1, axis=0), 0)
    for n in (1, 2, 4):
        below = below + jnp.where(sublane >= n, pltpu.roll(below, n, axis=0), 0)
    slot = jnp.where(mark == 1, count + below - 1, -1)
    region = (sublane * 128 + lane).astype(F32)
    tiles = []
    for z in range(subs):
        wide = jnp.concatenate([lab[z], jnp.full_like(lab[z], -2)], axis=1).astype(F32)
        for n in range(strips // 8):
            two = [jnp.broadcast_to(wide[2 * n + k : 2 * n + k + 1], (4, 128)) for k in range(2)]
            tiles.append(jnp.concatenate(two, axis=0))
    for s in range(OWNED_MOST):
        mine = jnp.max(jnp.where(slot == s, region, -1.0), axis=1, keepdims=True)
        mine = jnp.max(mine, axis=0, keepdims=True)
        for n in range(devices // 8):
            pick[s, pl.ds(8 * n, 8), :] = jnp.where(tiles[n] == mine, 1.0, 0.0)

    c0, c1, c2 = solve(moments_in(1, row1), SIGMA[1])

    def finish(q, sums):
        for p in OWN:
            for m in range(2):
                mode = at(mode_m, q + m, p) + (
                    c0 * at(r_m, q + m, p) + (c1 * at(a_m, q + m, p) + c2 * at(b_m, q + m, p))
                )
                put(mode_m, q + m, p, mode)
                summed(sums, m, [jnp.exp(at(off_m, q + m, p) + mode)])

    line = over_sublanes(closed(sum_blocks(TOP, BOTTOM, 2, 1, finish))[0])
    line = line + pltpu.roll(line, 64, axis=1)
    row2 = (line * (1.0 / (TILE * TILE)))[0:1]
    tell(2, row2)

    outs = []

    def write_out(i):
        def pair(m):
            row = 2 * m
            q = TOP + 8 * i + row
            x = jnp.concatenate([mode_m[q, 8:72, :], mode_m[q + 1, 8:72, :]], axis=0).T
            for g in range(8):
                upper, lower = x[8 * g : 8 * g + 8], x[64 + 8 * g : 72 + 8 * g]
                to = 512 * i + 64 * g + row
                st_o[pl.ds(to, 8, stride=8), :] = jnp.where(low_half, upper, pltpu.roll(lower, 64, axis=1))
                st_o[pl.ds(to + 1, 8, stride=8), :] = jnp.where(low_half, pltpu.roll(upper, 64, axis=1), lower)

        each(0, 4, pair)
        part = pl.ds(512 * i, 512)
        outs.append(pltpu.make_async_copy(st_o.at[part, :], mode_h.at[part, :], out_sem.at[i]))
        outs[-1].start()

    write_out(0)
    write_out(1)
    write_out(2)
    write_out(3)
    total = heard(2, row2)
    answer = zero
    for h in range(2):
        gathered = zero
        for s in range(8 * h, min(8 * h + 8, OWNED_MOST)):
            both = added([v * pick[s, pl.ds(8 * n, 8), :] for n, v in enumerate(total)])
            gathered = jnp.where(
                sublane == s - 8 * h, over_sublanes(both), gathered
            )
        flat = jnp.sum(gathered, axis=1, keepdims=True)
        answer = answer + jnp.where(lane == sublane + 8 * h, flat, 0.0)
    owned_ref[...] = over_sublanes(answer)[0:1, 0:OWNED_MOST]
    for copy in outs:
        copy.wait()


def solution(mesh):
    strips, subs = mesh.shape["strip"], mesh.shape["sub"]
    devices = strips * subs

    def tiled(x):
        return x.reshape(4, 8, 64, 128).transpose(0, 2, 1, 3).reshape(2048, 128)

    def body(counts, offset, kappa, labels, owner):
        field = pltpu.VMEM((SLOTS, PITCH, 128), F32)
        stage = pltpu.VMEM((2048, 128), F32)
        dma = pltpu.SemaphoreType.DMA
        anywhere = pl.BlockSpec(memory_space=pl.ANY)
        mode, owned = pl.pallas_call(
            lambda *refs: kernel((strips, subs), *refs),
            out_shape=(
                jax.ShapeDtypeStruct((2048, 128), F32),
                jax.ShapeDtypeStruct((1, OWNED_MOST), F32),
            ),
            in_specs=[anywhere] * 5,
            out_specs=(anywhere, pl.BlockSpec(memory_space=pltpu.VMEM)),
            scratch_shapes=[
                pltpu.VMEM((2048, 128), jnp.int32), stage, stage,
                field, field, field, field, field, field, field, field, field,
                pltpu.VMEM((6, 2, 8, 128), F32),
                pltpu.VMEM((36, 8, 128), F32),
                pltpu.VMEM((subs, 8, labels.shape[1]), jnp.int32),
                pltpu.VMEM((8, 128), jnp.int32),
                pltpu.VMEM((OWNED_MOST, devices, 128), F32),
                pltpu.VMEM((3, 1, 128), F32),
                pltpu.VMEM((3, devices, 128), F32),
                dma((12,)), dma((2,)), dma((16,)), dma((16,)), dma((36,)), dma((36,)),
                dma((subs,)), dma((subs,)), dma((3,)), dma((3,)), dma((4,)),
            ],
            compiler_params=pltpu.CompilerParams(
                collective_id=0, has_side_effects=True, vmem_limit_bytes=55000000
            ),
        )(tiled(counts), tiled(offset), tiled(kappa), pltpu.with_memory_space_constraint(labels, pltpu.HBM), pltpu.with_memory_space_constraint(owner.reshape(8, 128), pltpu.HBM))
        mode = mode.reshape(4, 64, 8, 128).transpose(0, 2, 1, 3).reshape(32, 8192)
        return mode, owned.reshape(OWNED_MOST)

    return jax.shard_map(
        body,
        mesh=mesh,
        in_specs=(P("strip", "sub"), P("strip", "sub"), P("strip", "sub"), P(None, "sub"), P()),
        out_specs=(P("strip", "sub"), P(("strip", "sub"))),
        check_vma=False,
    )
```

```python
import jax
import jax.numpy as jnp
from jax import lax
from jax.experimental import pallas as pl
from jax.experimental.pallas import tpu as pltpu
from jax.sharding import PartitionSpec as P

TILE = 128
OWNED_MOST = 15
MESH = pl.DeviceIdType.MESH
F32 = jnp.float32

ROWS, TOP, BOTTOM, SLOTS, DEEP = 32, 8, 40, 48, 5
PITCH = 80
OWN = tuple(range(8, 72, 8))
ALL = (1,) + OWN + (71,)
SHIFTS = (3.0, 40.0)
SIGMA = (1.0, 2.0**-27)
TINY = 3e-7


def kernel(
    dims, counts_h, offset_h, kappa_h, labels_h, owner_h, mode_h, owned_ref,
    st_c, st_o, st_k, off_m, kap_m, w_m, r_m, t_m, a_m, b_m, q_m, mode_m,
    pack, land, lab, own, pick, src, got,
    ld_sem, small_sem, row_s, row_r, edge_s, edge_r, lab_s, lab_r, sum_s, sum_r, out_sem,
):
    strips, subs = dims
    strip, sub = lax.axis_index("strip"), lax.axis_index("sub")
    core, chip = lax.rem(strip, 2), lax.div(strip, 2)
    devices = strips * subs
    me = sub * strips + strip
    up, down = lax.rem(strip + strips - 1, strips), lax.rem(strip + 1, strips)
    left, right = lax.rem(sub + subs - 1, subs), lax.rem(sub + 1, subs)
    first, last = strip == 0, strip == strips - 1

    side = 4 if strips == 32 else 2
    tall = strips // 2 // side

    def far(n, size):
        return min(n, size - n)

    def turned_by(x, n, size):
        return lax.rem(x + n, size) if n else x

    at_y = [turned_by(lax.div(chip, side), n, tall) for n in range(tall)]
    at_x = [turned_by(lax.rem(chip, side), n, side) for n in range(side)]
    at_z = [turned_by(sub, n, subs) for n in range(subs)]
    peers = []
    for dy, dx, dz, flip in sorted(
        (
            (y, x, z, f) for y in range(tall) for x in range(side) for z in range(subs)
            for f in range(2) if y or x or z or f
        ),
        key=lambda v: -far(v[0], tall) - far(v[1], side) - far(v[2], subs),
    ):
        core_ = 1 - core if flip else core
        peers.append(((at_y[dy] * side + at_x[dx]) * 2 + core_, at_z[dz]))

    def each(low, high, do):
        def step(k, carry):
            do(k)
            return carry

        lax.fori_loop(low, high, step, 0)

    barrier = pltpu.get_barrier_semaphore()
    for device in peers:
        pl.semaphore_signal(barrier, inc=1, device_id=device, device_id_type=MESH)

    order = (0, 3, 1, 2)
    loads = {}
    for i in order:
        for n, (hbm, stage) in enumerate(((offset_h, st_o), (counts_h, st_c), (kappa_h, st_k))):
            part = pl.ds(512 * i, 512)
            loads[i, n] = pltpu.make_async_copy(hbm.at[part, :], stage.at[part, :], ld_sem.at[3 * i + n])
            loads[i, n].start()
    load_owner = pltpu.make_async_copy(owner_h, own, small_sem.at[0])
    load_owner.start()
    load_labels = pltpu.make_async_copy(labels_h, lab.at[sub], small_sem.at[1])
    load_labels.start()

    lane = lax.broadcasted_iota(jnp.int32, (8, 128), 1)
    sublane = lax.broadcasted_iota(jnp.int32, (8, 128), 0)
    low_half = lane < 64
    zero = jnp.zeros((8, 128), F32)

    def relayout(i, wait=True):
        for n in range(3 if wait else 0):
            loads[i, n].wait()

        def pair(m):
            row = 2 * m

            def turned(stage):
                x = [
                    [
                        stage[pl.ds(512 * i + 64 * g + row + d, 8, stride=8), :].astype(F32)
                        for g in range(8)
                    ]
                    for d in range(2)
                ]
                upper = [jnp.where(low_half, x[0][g], pltpu.roll(x[1][g], 64, axis=1)) for g in range(8)]
                lower = [jnp.where(low_half, pltpu.roll(x[0][g], 64, axis=1), x[1][g]) for g in range(8)]
                return jnp.concatenate(upper + lower, axis=0).T

            off, cnt, kap = turned(st_o), turned(st_c), turned(st_k)
            for d in range(2):
                q = TOP + 8 * i + row + d
                part = slice(64 * d, 64 * d + 64)
                weight = jnp.exp(off[part])
                off_m[q, 8:72, :] = off[part]
                kap_m[q, 8:72, :] = kap[part] + 4.0
                w_m[q, 8:72, :] = 10.0 * weight
                r_m[q, 8:72, :] = cnt[part] - weight

        each(0, 4, pair)

    def remote(src, dst, send, recv, device):
        return pltpu.make_async_remote_copy(
            src_ref=src, dst_ref=dst, send_sem=send, recv_sem=recv,
            device_id=device, device_id_type=MESH,
        )

    def row_copies(field, n, low, high):
        many = high - low

        def rows(q):
            return field.at[pl.ds(q, many), pl.ds(8, 64), :]

        return [
            remote(rows(TOP + low), rows(BOTTOM + low), row_s.at[2 * n], row_r.at[2 * n], (up, sub)),
            remote(
                rows(BOTTOM - high), rows(TOP - high),
                row_s.at[2 * n + 1], row_r.at[2 * n + 1], (down, sub),
            ),
        ]

    def edge_copies(n):
        made = []
        for to, beside in ((1, left), (0, right)):
            for m, device in enumerate(((strip, beside), (down, beside), (up, beside))):
                k = 6 * n + 3 * to + m
                made.append(
                    remote(pack.at[n, to], land.at[k], edge_s.at[k], edge_r.at[k], device)
                )
        return made

    def pack_field(field, n):
        tiles = [zero, zero]
        for q in range(TOP, BOTTOM):
            for to, p, l in ((1, 8, 0), (0, 64, 127)):
                moved = pltpu.roll(field[q, p : p + 8, :], (q - l) % 128, axis=1)
                tiles[to] = jnp.where(lane == q, moved, tiles[to])
        for to in range(2):
            pack[n, to] = tiles[to]

    def pack_inputs():
        for to, g, keep in ((1, 0, slice(0, 8)), (0, 63, slice(120, 128))):
            tiles = []
            for stage in (st_o, st_c, st_k):
                x = [stage[pl.ds(512 * i + 8 * g, 8), :].astype(F32) for i in range(4)]
                tiles.append(jnp.concatenate([zero] + x + [zero] * 11, axis=0).T[keep])
            pack[0, to] = tiles[0]
            pack[1, to] = tiles[1] - jnp.exp(tiles[0])
            pack[2, to] = tiles[2]

    def landed(n, to):
        k = 6 * n + 3 * to
        return jnp.where(
            lane < TOP, pltpu.roll(land[k + 1], 96, axis=1),
            jnp.where(lane < BOTTOM, land[k], pltpu.roll(land[k + 2], 32, axis=1)),
        )

    def start(copies):
        for copy in copies:
            copy.start()

    def arrived(copies):
        for copy in copies:
            copy.wait_recv()

    def sent(copies):
        for copy in copies:
            copy.wait_send()

    left_open = jnp.where(sub > 0, 1.0, 0.0).astype(F32)
    right_open = jnp.where(sub < subs - 1, 1.0, 0.0).astype(F32)
    left_shut = jnp.where((lane == 0) & (sublane < 7), 1.0 - left_open, 0.0) > 0.5
    right_shut = jnp.where((lane == 127) & (sublane >= 1), 1.0 - right_open, 0.0) > 0.5

    def at(field, q, p):
        return field[q, p : p + 8, :]

    def put(field, q, p, value):
        field[q, p : p + 8, :] = value

    def k_tile(field, q, p, many):
        window = [at(field, q - 1 + m, p) for m in range(many + 2)]
        made = []
        for m in range(many):
            beside = at(field, q + m, p - 1) + at(field, q + m, p + 1)
            value = at(kap_m, q + m, p) * window[m + 1] - ((window[m] + window[m + 2]) + beside)
            if p == ALL[0]:
                value = jnp.where(left_shut, 0.0, value)
            if p == ALL[-1]:
                value = jnp.where(right_shut, 0.0, value)
            made.append(value)
        return made, window[1:-1]

    def blank(field, low, high):
        nothing = jnp.zeros((PITCH, 128), F32)

        @pl.when(first)
        def _():
            for q in range(low, TOP):
                field[q] = nothing

        @pl.when(last)
        def _():
            for q in range(BOTTOM, high):
                field[q] = nothing

    def blocks(low, high, many, do):
        each(0, (high - low) // many, lambda n: do(low + many * n))

    def k_block(field, out, q, many, tiles=ALL, scale=1.0):
        for p in tiles:
            made, _ = k_tile(field, q, p, many)
            for m in range(many):
                put(out, q + m, p, made[m] if scale == 1.0 else scale * made[m])

    def apply_k(field, out, low, high, many, tiles=ALL, scale=1.0):
        blocks(low, high, many, lambda q: k_block(field, out, q, many, tiles, scale))

    def summed(sums, n, terms):
        sums[n % 2] = [x + y for x, y in zip(sums[n % 2], terms)]

    def shift_block(base, out, q, many, shift, sigma, products, sums, counted):
        for p in ALL:
            made, _ = k_tile(t_m, q, p, many)
            for m in range(many):
                value, weight = at(base, q + m, p), at(w_m, q + m, p)
                got = made[m] + (weight - sigma * shift) * value
                put(out, q + m, p, got)
                if m in counted and p in OWN:
                    summed(sums, m + p // 8, products(value, got))

    def energy_block(q, many, sigma, sums):
        for p in OWN:
            made, values = k_tile(b_m, q, p, many)
            for m in range(many):
                square = made[m] * made[m]
                square = square if sigma == 1.0 else sigma * square
                summed(sums, m + p // 8, [square + at(w_m, q + m, p) * (values[m] * values[m])])

    def sum_blocks(low, high, many, count, do):
        def some(n, carry):
            sums = [list(carry[:count]), list(carry[count:])]
            do(low + many * n, sums)
            return tuple(sums[0] + sums[1])

        total = lax.fori_loop(0, (high - low) // many, some, (zero,) * (2 * count))
        return [list(total[:count]), list(total[count:])]

    def inject(field, edges, low, high):
        for q in range(low, high):
            x = at(field, q, 64)
            ghost = jnp.where(low_half, pltpu.roll(x, 65, axis=1), pltpu.roll(x, 64, axis=1))
            put(field, q, 0, jnp.where(lane == 0, pltpu.roll(edges[0], (128 - q) % 128, axis=1), ghost))
            x = at(field, q, 8)
            ghost = jnp.where(low_half, pltpu.roll(x, 64, axis=1), pltpu.roll(x, 63, axis=1))
            put(field, q, 72, jnp.where(lane == 127, pltpu.roll(edges[1], 127 - q, axis=1), ghost))

    def inject_halo(field, edges, near_=0, far_=DEEP):
        inject(field, edges, TOP - far_, TOP - near_)
        inject(field, edges, BOTTOM + near_, BOTTOM + far_)

    def tell(u, row):
        src[u] = row
        for device in peers:
            remote(src.at[u], got.at[u, pl.ds(me, 1), :], sum_s.at[u], sum_r.at[u], device).start()

    def heard(u, row):
        rows = got.at[u, pl.ds(0, devices - 1), :]
        remote(rows, rows, sum_s.at[u], sum_r.at[u], peers[0]).wait()
        made = []
        for n in range(devices // 8):
            made.append(jnp.where(sublane + 8 * n == me, row, got[u, pl.ds(8 * n, 8), :]))
        return made

    def added(terms):
        while len(terms) > 1:
            terms = [a + b for a, b in zip(terms[::2], terms[1::2])] + terms[len(terms) // 2 * 2 :]
        return terms[0]

    def over_sublanes(v):
        for n in (4, 2, 1):
            v = v + pltpu.roll(v, n, axis=0)
        return v

    def moments_out(u, sums):
        message = zero
        for n, v in enumerate(sums):
            message = jnp.where(sublane == n, over_sublanes(v), message)
        flat = jnp.sum(message, axis=1, keepdims=True)
        row = over_sublanes(jnp.where(lane == sublane, flat, 0.0))[0:1]
        tell(u, row)
        return row

    def moments_in(u, row):
        total = over_sublanes(added(heard(u, row)))
        return [jnp.broadcast_to(total[:, n : n + 1], (8, 128)) for n in range(6)]

    def solve(moments, sigma):
        g00, g01, g11, g12, g22, h22 = moments
        inverse = 1.0 / sigma
        t0, t1 = SHIFTS
        g02 = g11 + (sigma * (t0 - t1)) * g01
        a00 = inverse * g01 + t0 * g00
        a01 = inverse * g11 + t0 * g01
        a02 = inverse * g12 + t0 * g02
        a11 = inverse * g12 + t1 * g11
        a12 = inverse * g22 + t1 * g12
        a22 = inverse * h22
        i0 = 1.0 / a00
        l10, l20 = a01 * i0, a02 * i0
        d1, u12 = a11 - l10 * a01, a12 - l10 * a02
        i1 = jnp.where(d1 > TINY * a11, 1.0 / d1, 0.0)
        l21 = u12 * i1
        d2 = a22 - l20 * a02 - l21 * u12
        i2 = jnp.where(d2 > TINY * a22, 1.0 / d2, 0.0)
        y0 = 10.0 * g00
        y1 = 10.0 * g01 - l10 * y0
        y2 = 10.0 * g02 - l20 * y0 - l21 * y1
        c2 = y2 * i2
        c1 = y1 * i1 - l21 * c2
        c0 = y0 * i0 - l10 * c1 - l20 * c2
        return c0, c1, c2

    relayout(order[0])
    relayout(order[1])
    for i in (1, 2):
        for n in range(3):
            loads[i, n].wait()
    pack_inputs()
    pl.semaphore_wait(barrier, len(peers))
    rims = edge_copies(0) + edge_copies(1) + edge_copies(2)
    start(rims)
    halo = row_copies(r_m, 0, 0, 5) + row_copies(kap_m, 2, 0, 4) + row_copies(off_m, 1, 0, 3)
    start(halo)
    rest = row_copies(off_m, 6, 3, 5) + row_copies(kap_m, 5, 4, 6)
    start(rest)
    load_labels.wait()

    def label_copy(k, arriving):
        z = lax.rem(sub + k, subs)
        held = z if arriving else sub
        return remote(labels_h, lab.at[held], lab_s.at[k], lab_r.at[held], (strip, z))

    for k in range(1, subs):
        label_copy(k, False).start()
    relayout(order[2], False)
    relayout(order[3], False)
    alive = (left_open, right_open)
    arrived(rims)
    e_off = [landed(0, to) for to in range(2)]
    e_r = [landed(1, to) * alive[to] for to in range(2)]
    e_kap = [landed(2, to) + 4.0 for to in range(2)]
    e_w = [10.0 * jnp.exp(v) for v in e_off]
    for field, edges in ((kap_m, e_kap), (w_m, e_w), (r_m, e_r)):
        inject(field, edges, TOP, BOTTOM)

    def of_a(r, a):
        return r * r, r * a, a * a

    def of_b(a, b):
        return a * b, b * b

    def closed(sums):
        return [x + y for x, y in zip(*sums)]

    def a_block(q, many, n, sums, counted):
        shift_block(r_m, a_m, q, many, SHIFTS[0], SIGMA[n], of_a, sums, counted)

    def b_block(q, many, n, sums, counted):
        shift_block(a_m, b_m, q, many, SHIFTS[1], SIGMA[n], of_b, sums, counted)

    apply_k(r_m, t_m, 9, 39, 6)
    sums_a = sum_blocks(10, 38, 4, 3, lambda q, sums: a_block(q, 4, 0, sums, range(4)))
    a_rows = row_copies(a_m, 3, 3, 5)
    start(a_rows)
    apply_k(a_m, t_m, 11, 35, 4)
    k_block(a_m, t_m, 35, 2)
    sums_b = sum_blocks(12, 36, 4, 2, lambda q, sums: b_block(q, 4, 0, sums, range(4)))
    b_rows = row_copies(b_m, 7, 4, 7)
    start(b_rows)
    sums_e = sum_blocks(13, 33, 4, 1, lambda q, sums: energy_block(q, 4, 1.0, sums))
    energy_block(33, 2, 1.0, sums_e)
    inject(off_m, e_off, TOP, BOTTOM)
    arrived(halo)
    for q in (5, 6, 7, 40, 41, 42):
        for p in OWN:
            put(w_m, q, p, 10.0 * jnp.exp(at(off_m, q, p)))
    inject_halo(kap_m, e_kap, 0, 4)
    inject_halo(w_m, e_w)
    inject_halo(r_m, e_r)
    blank(r_m, TOP - DEEP, BOTTOM + DEEP)
    k_block(r_m, t_m, 4, 5)
    k_block(r_m, t_m, 39, 5)
    blank(t_m, 4, 44)
    a_block(5, 5, 0, sums_a, (3, 4))
    a_block(38, 5, 0, sums_a, (0, 1))
    blank(a_m, 5, 43)
    k_block(a_m, t_m, 6, 5)
    k_block(a_m, t_m, 37, 5)
    blank(t_m, 6, 42)
    b_block(7, 5, 0, sums_b, (1, 2, 3, 4))
    b_block(36, 5, 0, sums_b, (0, 1, 2, 3))
    blank(b_m, 7, 41)
    outer = row_copies(b_m, 4, 1, 4)
    start(outer)
    b_rows = b_rows + outer
    energy_block(8, 5, 1.0, sums_e)
    energy_block(35, 5, 1.0, sums_e)
    pack_field(a_m, 3)
    pack_field(b_m, 4)
    ab_rims = edge_copies(3) + edge_copies(4)
    start(ab_rims)
    row0 = moments_out(0, closed(sums_a) + closed(sums_b) + closed(sums_e))
    moving = a_rows + b_rows + ab_rims
    arrived(rest)
    inject_halo(off_m, e_off)
    inject_halo(kap_m, e_kap, 4, 6)

    def second_k(q, many, tiles=ALL):
        for p in tiles:
            made, _ = k_tile(t_m, q, p, many)
            for m in range(many):
                put(q_m, q + m, p, made[m])

    apply_k(b_m, t_m, 9, 39, 6, OWN)
    blocks(10, 38, 4, lambda q: second_k(q, 4, OWN[1:-1]))
    arrived(ab_rims)
    e_b = [landed(4, to) * alive[to] for to in range(2)]
    inject(b_m, e_b, TOP, BOTTOM)
    apply_k(b_m, t_m, 9, 39, 6, ALL[::9])
    blocks(10, 38, 4, lambda q: second_k(q, 4, ALL[:2] + ALL[-2:]))
    inject(a_m, [landed(3, to) for to in range(2)], TOP, BOTTOM)
    arrived(a_rows)
    inject_halo(a_m, [landed(3, to) for to in range(2)])
    arrived(b_rows)
    inject_halo(b_m, e_b, 0, 7)
    blank(b_m, 1, 47)
    for q in (2, 39):
        k_block(b_m, t_m, q, 7)
    blank(t_m, 2, 46)
    for q in (3, 38):
        second_k(q, 7)
    sent(moving)
    sent(halo)

    c0, c1, c2 = solve(moments_in(0, row0), SIGMA[0])
    d0, d1, d2 = 0.1 * c0, 0.1 * c1, 0.1 * c2

    def renew(off, weight, r, a, b, qb):
        step = c0 * r + (c1 * a + c2 * b)
        q_mode = d0 * (a + (SHIFTS[0] - weight) * r) + (d1 * (b + (SHIFTS[1] - weight) * a) + d2 * qb)
        fresh = jnp.exp(off + step)
        return step, (10.0 * SIGMA[1]) * fresh, ((r + 0.1 * weight) - fresh) - q_mode

    def renew_rows(q, many, keep):
        for p in range(0, PITCH, 8):
            for m in range(many):
                off = at(off_m, q + m, p)
                weight = at(w_m, q + m, p) if keep else 10.0 * jnp.exp(off)
                step, fresh, gradient = renew(off, weight, *(at(f, q + m, p) for f in (r_m, a_m, b_m, q_m)))
                if p == 0:
                    gradient = jnp.where(lane == 0, jnp.where(sub > 0, gradient, 0.0), gradient)
                elif p == 72:
                    gradient = jnp.where(lane == 127, jnp.where(sub < subs - 1, gradient, 0.0), gradient)
                elif keep:
                    put(mode_m, q + m, p, step)
                put(w_m, q + m, p, fresh)
                put(r_m, q + m, p, gradient)

    blocks(TOP, BOTTOM, 2, lambda q: renew_rows(q, 2, True))
    each(TOP - DEEP, TOP, lambda q: renew_rows(q, 1, False))
    each(BOTTOM, BOTTOM + DEEP, lambda q: renew_rows(q, 1, False))
    blank(r_m, TOP - DEEP, BOTTOM + DEEP)

    apply_k(r_m, t_m, 4, 44, 4, ALL, SIGMA[1])
    blank(t_m, 4, 44)
    sums_a = sum_blocks(8, 40, 4, 3, lambda q, sums: a_block(q, 4, 1, sums, range(4)))
    a_block(5, 3, 1, None, ())
    a_block(40, 3, 1, None, ())
    blank(a_m, 5, 43)
    apply_k(a_m, t_m, 6, 42, 4, ALL, SIGMA[1])
    blank(t_m, 6, 42)
    sums_b = sum_blocks(8, 40, 4, 2, lambda q, sums: b_block(q, 4, 1, sums, range(4)))
    b_block(7, 1, 1, None, ())
    b_block(40, 1, 1, None, ())
    blank(b_m, 7, 41)
    sums_e = sum_blocks(8, 40, 4, 1, lambda q, sums: energy_block(q, 4, SIGMA[1], sums))
    row1 = moments_out(1, closed(sums_a) + closed(sums_b) + closed(sums_e))

    sent(rims)
    sent(rest)
    for k in range(1, subs):
        label_copy(k, True).wait()
    load_owner.wait()
    myself = strip * subs + sub
    mark = jnp.where(own[...] == myself, 1, 0)
    count = mark
    for n in (1, 2, 4, 8, 16, 32, 64):
        count = count + jnp.where(lane >= n, pltpu.roll(count, n, axis=1), 0)
    whole = jnp.broadcast_to(count[:, 127:128], (8, 128))
    below = jnp.where(sublane >= 1, pltpu.roll(whole, 1, axis=0), 0)
    for n in (1, 2, 4):
        below = below + jnp.where(sublane >= n, pltpu.roll(below, n, axis=0), 0)
    slot = jnp.where(mark == 1, count + below - 1, -1)
    region = (sublane * 128 + lane).astype(F32)
    tiles = []
    for z in range(subs):
        wide = jnp.concatenate([lab[z], jnp.full_like(lab[z], -2)], axis=1).astype(F32)
        for n in range(strips // 8):
            two = [jnp.broadcast_to(wide[2 * n + k : 2 * n + k + 1], (4, 128)) for k in range(2)]
            tiles.append(jnp.concatenate(two, axis=0))
    for s in range(OWNED_MOST):
        mine = jnp.max(jnp.where(slot == s, region, -1.0), axis=1, keepdims=True)
        mine = jnp.max(mine, axis=0, keepdims=True)
        for n in range(devices // 8):
            pick[s, pl.ds(8 * n, 8), :] = jnp.where(tiles[n] == mine, 1.0, 0.0)

    c0, c1, c2 = solve(moments_in(1, row1), SIGMA[1])

    def finish(q, sums):
        for p in OWN:
            for m in range(2):
                mode = at(mode_m, q + m, p) + (
                    c0 * at(r_m, q + m, p) + (c1 * at(a_m, q + m, p) + c2 * at(b_m, q + m, p))
                )
                put(mode_m, q + m, p, mode)
                summed(sums, m, [jnp.exp(at(off_m, q + m, p) + mode)])

    line = over_sublanes(closed(sum_blocks(TOP, BOTTOM, 2, 1, finish))[0])
    line = line + pltpu.roll(line, 64, axis=1)
    row2 = (line * (1.0 / (TILE * TILE)))[0:1]
    tell(2, row2)

    outs = []

    def write_out(i):
        def pair(m):
            row = 2 * m
            q = TOP + 8 * i + row
            x = jnp.concatenate([mode_m[q, 8:72, :], mode_m[q + 1, 8:72, :]], axis=0).T
            for g in range(8):
                upper, lower = x[8 * g : 8 * g + 8], x[64 + 8 * g : 72 + 8 * g]
                to = 512 * i + 64 * g + row
                st_o[pl.ds(to, 8, stride=8), :] = jnp.where(low_half, upper, pltpu.roll(lower, 64, axis=1))
                st_o[pl.ds(to + 1, 8, stride=8), :] = jnp.where(low_half, pltpu.roll(upper, 64, axis=1), lower)

        each(0, 4, pair)
        part = pl.ds(512 * i, 512)
        outs.append(pltpu.make_async_copy(st_o.at[part, :], mode_h.at[part, :], out_sem.at[i]))
        outs[-1].start()

    write_out(0)
    write_out(1)
    write_out(2)
    write_out(3)
    total = heard(2, row2)
    answer = zero
    for h in range(2):
        gathered = zero
        for s in range(8 * h, min(8 * h + 8, OWNED_MOST)):
            both = added([v * pick[s, pl.ds(8 * n, 8), :] for n, v in enumerate(total)])
            gathered = jnp.where(
                sublane == s - 8 * h, over_sublanes(both), gathered
            )
        flat = jnp.sum(gathered, axis=1, keepdims=True)
        answer = answer + jnp.where(lane == sublane + 8 * h, flat, 0.0)
    owned_ref[...] = over_sublanes(answer)[0, 0:OWNED_MOST]
    for copy in outs:
        copy.wait()


def solution(mesh):
    strips, subs = mesh.shape["strip"], mesh.shape["sub"]
    devices = strips * subs

    def tiled(x):
        return x.reshape(4, 8, 64, 128).transpose(0, 2, 1, 3).reshape(2048, 128)

    def body(counts, offset, kappa, labels, owner):
        field = pltpu.VMEM((SLOTS, PITCH, 128), F32)
        stage = pltpu.VMEM((2048, 128), F32)
        dma = pltpu.SemaphoreType.DMA
        anywhere = pl.BlockSpec(memory_space=pl.ANY)
        mode, owned = pl.pallas_call(
            lambda *refs: kernel((strips, subs), *refs),
            out_shape=(
                jax.ShapeDtypeStruct((2048, 128), F32),
                jax.ShapeDtypeStruct((OWNED_MOST,), F32),
            ),
            in_specs=[anywhere] * 5,
            out_specs=(anywhere, pl.BlockSpec(memory_space=pltpu.VMEM)),
            scratch_shapes=[
                pltpu.VMEM((2048, 128), jnp.int32), stage, stage,
                field, field, field, field, field, field, field, field, field,
                pltpu.VMEM((6, 2, 8, 128), F32),
                pltpu.VMEM((36, 8, 128), F32),
                pltpu.VMEM((subs, 8, labels.shape[1]), jnp.int32),
                pltpu.VMEM((8, 128), jnp.int32),
                pltpu.VMEM((OWNED_MOST, devices, 128), F32),
                pltpu.VMEM((3, 1, 128), F32),
                pltpu.VMEM((3, devices, 128), F32),
                dma((12,)), dma((2,)), dma((16,)), dma((16,)), dma((36,)), dma((36,)),
                dma((subs,)), dma((subs,)), dma((3,)), dma((3,)), dma((4,)),
            ],
            compiler_params=pltpu.CompilerParams(
                collective_id=0, has_side_effects=True, vmem_limit_bytes=55000000
            ),
        )(tiled(counts), tiled(offset), tiled(kappa), pltpu.with_memory_space_constraint(labels, pltpu.HBM), pltpu.with_memory_space_constraint(owner.reshape(8, 128), pltpu.HBM))
        mode = mode.reshape(4, 64, 8, 128).transpose(0, 2, 1, 3).reshape(32, 8192)
        return mode, owned

    return jax.shard_map(
        body,
        mesh=mesh,
        in_specs=(P("strip", "sub"), P("strip", "sub"), P("strip", "sub"), P(None, "sub"), P()),
        out_specs=(P("strip", "sub"), P(("strip", "sub"))),
        check_vma=False,
    )
```
